32 devices in a mesh: row: 8 (over z, x), col: 4 (over y, core).
Axes of the slice: x: 2, y: 2, z: 4, core: 2. Of those that a mesh axis runs over, the one named last changes fastest.
Arguments:
- links: bfloat16 [2048, 2048], P('row', 'col'), may hold values from 0 to 3, as said below
- tiles: int32 [16, 16], P('row', 'col'), may hold values from 0 to 1
- local_links: bfloat16 [2048, 64], P(('col', 'row')), may hold values from 0 to 2, as said below
- host_ids: int32 [2048], replicated, may hold values from 0 to 127, as said below
- dangling: int32 [2048], replicated, may hold values 0 or 1
- teleport: float32 [2048, 128], P(('col', 'row')), may hold values from 0.1 to 10
Outputs:
- ranks: float32 [2048, 128], P(('row', 'col'))
The draws below stay inside these ranges and needn't reach their ends.
Inputs may be any that keep to these rules, and one draw needn't show every extreme that they name: `links`: small whole link counts. `local_links`: small whole link counts. `host_ids`: the pages of piece q form exactly 4 hosts, numbered q * 4 onwards in page order; each host is a run of consecutive pages.
All inputs are finite; a program needn't handle non-finite values.
Results may differ from the reference program's by a relative error of at most 0.0045.
Values may be sent and summed in bfloat16 or wider, within the bound.
No kernel may reach another device: no remote copies, remote signals or barrier semaphores. Data moves between devices by JAX's collectives and lax.ppermute only.
A program may use at most 64 MiB of HBM per device.

```python
import math
import jax
import jax.numpy as jnp
from jax import lax

PIECE = 64
TILE = 128
HOSTS_PIECE = 4
LOCAL_ITERS = 2
HOST_ITERS = 3
TOPICS = 128
PAGES = 2048
HOSTS = 128


def draw_links(key, part):
    first, second = jax.random.split(jax.random.fold_in(key, 11))
    present = jax.random.randint(first, (PAGES, PAGES), 0, TILE) < 2
    counts = jax.random.randint(second, (PAGES, PAGES), 1, 4)
    return jnp.where(present, counts, 0).astype(jnp.float32).astype(jnp.bfloat16)


def draw_tiles(key, part):
    count = PAGES // TILE
    first, second = jax.random.split(jax.random.fold_in(key, 23))
    level = jax.random.randint(first, (count // 8, count // 8), 1, 9)
    group = jnp.arange(count, dtype=jnp.int32) // 8
    density = level[group[:, None], group[None, :]]
    return (jax.random.randint(second, (count, count), 0, 2 * count) < density).astype(jnp.int32)


def draw_local_links(key, part):
    first, second = jax.random.split(jax.random.fold_in(key, 37))
    present = jax.random.randint(first, (PAGES, PIECE), 0, 4) == 0
    counts = jax.random.randint(second, (PAGES, PIECE), 1, 3)
    return jnp.where(present, counts, 0).astype(jnp.float32).astype(jnp.bfloat16)


def draw_host_ids(key, part):
    count = PAGES // PIECE
    scores = jax.random.randint(jax.random.fold_in(key, 41), (count, PIECE - 1), 0, 1 << 20) * PIECE + jnp.arange(PIECE - 1, dtype=jnp.int32)[None, :]
    order = jnp.argsort(scores, axis=1, stable=True)
    placed = jnp.argsort(order, axis=1, stable=True)
    cuts = (placed < HOSTS_PIECE - 1).astype(jnp.int32)
    within = jnp.cumsum(jnp.concatenate([jnp.zeros((count, 1), jnp.int32), cuts], axis=1), axis=1)
    return (within + jnp.arange(count, dtype=jnp.int32)[:, None] * HOSTS_PIECE).reshape(PAGES).astype(jnp.int32)


def plant(result, key, low, largest):
    shape = result.shape
    spot = [jax.random.randint(jax.random.fold_in(key, axis), (), 0, shape[axis]) for axis in range(len(shape))]
    result = result.at[tuple(spot)].set(low)
    longest = shape.index(max(shape))
    spot[longest] = (spot[longest] + 1) % shape[longest]
    return result.at[tuple(spot)].set(largest)


def level_of(stream_key, shape, shards, least, top_value):
    gain = 1.0
    for position, shards_of in shards:
        draws = jax.random.uniform(jax.random.fold_in(jax.random.fold_in(stream_key, 6), position), (shards_of,), jnp.float32, least / len(shards), top_value / len(shards))
        gain = gain * jnp.repeat(jnp.exp(draws), shape[position] // shards_of).reshape((-1,) + (1,) * (len(shape) - 1 - position))
    return gain


def setup_inputs(seed: int = 0) -> dict:
    arg_keys = jax.random.split(jax.random.key(seed), 7)
    return {
        "links": draw_links(jax.random.fold_in(arg_keys[6], 71), 0),
        "tiles": draw_tiles(jax.random.fold_in(arg_keys[6], 71), 0),
        "local_links": draw_local_links(jax.random.fold_in(arg_keys[6], 71), 0),
        "host_ids": draw_host_ids(jax.random.fold_in(arg_keys[6], 71), 0),
        "dangling": plant((jax.random.randint(arg_keys[4], (PAGES,), 0, 8) < 1).astype(jnp.int32), jax.random.fold_in(arg_keys[4], 1), 0, 1),
        "teleport": jnp.clip(jnp.exp(math.log(10.0) - 4.6051702 * jax.random.uniform(arg_keys[5], (PAGES, TOPICS), jnp.float32) ** level_of(arg_keys[5], (PAGES, TOPICS), ((0, 32),), -0.2, 0.2)), 0.1, 10.0),
    }


damping = 0.85
highest = lax.Precision.HIGHEST


def local_ranks(local_links, hosts, dangling, teleport, first_host):
    member = ((hosts - first_host[:, None])[:, :, None] == jnp.arange(HOSTS_PIECE, dtype=jnp.int32)[None, None, :]).astype(jnp.float32)
    same = (hosts[:, :, None] == hosts[:, None, :]).astype(jnp.float32)
    follow = (1 - dangling).astype(jnp.float32)
    inside = local_links.astype(jnp.float32) * same * follow[:, None, :]
    inward = jnp.sum(inside, axis=1)
    live = inward > 0
    inverse = jnp.where(live, 1.0 / jnp.where(live, inward, 1.0), 0.0)
    sizes = jnp.sum(member, axis=1)
    page_size = jnp.einsum('npg,ng->np', member, sizes, precision=highest)
    host_tele = jnp.einsum('npg,npk->ngk', member, teleport, precision=highest)
    page_tele = jnp.einsum('npg,ngk->npk', member, host_tele, precision=highest)
    restart = page_size[:, :, None] * teleport / page_tele
    ranks = jnp.ones(teleport.shape, jnp.float32)
    for step in range(LOCAL_ITERS):
        flow = jnp.einsum('npq,nqk->npk', inside, ranks * inverse[:, :, None], precision=highest)
        lost = jnp.einsum('npg,npk->ngk', member, jnp.where(live[:, :, None], 0.0, ranks), precision=highest)
        spread = jnp.einsum('npg,ngk->npk', member, lost, precision=highest) / page_size[:, :, None]
        ranks = damping * (flow + spread) + (1 - damping) * restart
    return ranks, member, inside, inward


def inter_rows(links, tiles, host_ids, dangling, start, count):
    rows = lax.dynamic_slice_in_dim(links, start, count, 0)
    tile_rows = lax.dynamic_slice_in_dim(tiles, start // TILE, count // TILE, 0)
    width = links.shape[1]
    stored = jnp.broadcast_to((tile_rows > 0)[:, None, :, None], (count // TILE, TILE, width // TILE, TILE)).reshape(count, width)
    host_rows = lax.dynamic_slice_in_dim(host_ids, start, count, 0)
    valid = stored & (host_rows[:, None] != host_ids[None, :]) & (dangling == 0)[None, :]
    return jnp.where(valid, rows, jnp.zeros((), jnp.bfloat16))


def reference(links, tiles, local_links, host_ids, dangling, teleport):
    pages = PAGES
    pieces = pages // PIECE
    height = min(1024, pages)
    starts = jnp.arange(pages // height, dtype=jnp.int32) * height

    def column_sums(start):
        return jnp.sum(inter_rows(links, tiles, host_ids, dangling, start, height).astype(jnp.float32), axis=0)

    outward = jnp.sum(lax.map(column_sums, starts), axis=0)
    ranks, member, inside, inward = local_ranks(local_links.reshape(pieces, PIECE, PIECE), host_ids.reshape(pieces, PIECE), dangling.reshape(pieces, PIECE), teleport.reshape(pieces, PIECE, TOPICS), jnp.arange(pieces, dtype=jnp.int32) * HOSTS_PIECE)
    degree = inward + outward.reshape(pieces, PIECE)
    has_out = degree > 0
    inverse_degree = jnp.where(has_out, 1.0 / jnp.where(has_out, degree, 1.0), 0.0)
    scaled = (ranks * inverse_degree[:, :, None]).astype(jnp.bfloat16)
    means = jnp.mean(scaled.astype(jnp.float32), axis=2).astype(jnp.bfloat16)
    spread_weight = member * means.astype(jnp.float32)[:, :, None]

    def host_block(start):
        edges = inter_rows(links, tiles, host_ids, dangling, start, height).astype(jnp.float32).reshape(height, pieces, PIECE)
        to_hosts = jnp.einsum('iqj,qjh->iqh', edges, spread_weight, precision=highest).reshape(height // PIECE, PIECE, HOSTS)
        row_member = lax.dynamic_slice_in_dim(member, start // PIECE, height // PIECE, 0)
        return jnp.einsum('pig,pih->pgh', row_member, to_hosts, precision=highest).reshape(height // PIECE * HOSTS_PIECE, HOSTS)

    weights = lax.map(host_block, starts).reshape(HOSTS, HOSTS)
    out_weight = jnp.sum(weights, axis=0)
    linked = out_weight > 0
    norm = jnp.where(linked[None, :], weights / jnp.where(linked, out_weight, 1.0)[None, :], 0.0)
    loose = jnp.where(linked, 0.0, 1.0)
    host_rank = jnp.ones((HOSTS,), jnp.float32)
    for step in range(HOST_ITERS):
        host_rank = damping * (jnp.dot(norm, host_rank, precision=highest) + jnp.sum(loose * host_rank) / HOSTS) + (1 - damping)
    page_weight = jnp.einsum('npg,ng->np', member, host_rank.reshape(pieces, HOSTS_PIECE), precision=highest)
    start_rank = ranks * page_weight[:, :, None]
    sources = (scaled.astype(jnp.float32) * page_weight[:, :, None]).astype(jnp.bfloat16)
    mass = jnp.sum(jnp.where(has_out[:, :, None], 0.0, start_rank), axis=(0, 1))
    tele_total = jnp.sum(teleport, axis=0)
    own = damping * jnp.einsum('npq,nqk->npk', inside, sources.astype(jnp.float32), precision=highest)
    own = own + (1 - damping) * pages * teleport.reshape(pieces, PIECE, TOPICS) / tele_total
    own = own.astype(jnp.bfloat16).reshape(pages, TOPICS)
    flat_sources = sources.reshape(pages, TOPICS)

    def inflow(start):
        edges = inter_rows(links, tiles, host_ids, dangling, start, height)
        return jnp.dot(edges, flat_sources, preferred_element_type=jnp.float32)

    flows = lax.map(inflow, starts).reshape(pages, TOPICS)
    return damping * flows + own.astype(jnp.float32) + damping * mass / pages
```

```python
import functools

import jax
import jax.numpy as jnp
from jax import lax
from jax.experimental import pallas as pl
from jax.experimental.pallas import tpu as pltpu
from jax.sharding import PartitionSpec as P

HOSTS_PIECE = 4
LOCAL_ITERS = 2
HOST_ITERS = 3
LANES = 128

damping = 0.85
f32 = jnp.float32
bf16 = jnp.bfloat16

VMEM = pl.BlockSpec(memory_space=pltpu.VMEM)
SMEM = pl.BlockSpec(memory_space=pltpu.SMEM)


def iota(shape, axis):
    return lax.broadcasted_iota(jnp.int32, shape, axis)


def mm(a, b):
    return jnp.dot(a, b, preferred_element_type=f32)


def mm_nt(a, b):
    return lax.dot_general(a, b, (((1,), (1,)), ((), ())), preferred_element_type=f32)


def mm_tn(a, b):
    return lax.dot_general(a, b, (((0,), (0,)), ((), ())), preferred_element_type=f32)


def split(x):
    high = x.astype(bf16)
    return high, (x - high.astype(f32)).astype(bf16)


def members(hosts_row, first, count):
    return hosts_row == first + iota((count, hosts_row.shape[1]), 0)


class Sizes:
    def __init__(self, rows, cols, links, tiles, local_links, teleport, pages):
        self.rows, self.cols, self.pages = rows, cols, pages
        self.height, self.width = links
        self.piece = local_links[0]
        self.topics = teleport[1]
        self.tile = self.height // tiles[0]
        self.tile_rows, self.units = tiles
        self.pair = self.tile // self.piece
        self.unit_hosts = self.pair * HOSTS_PIECE
        self.hosts = HOSTS_PIECE * rows * cols
        self.column_hosts = HOSTS_PIECE * rows
        self.row_hosts = HOSTS_PIECE * cols
        self.packed = self.piece * self.piece // LANES
        self.at_links = self.piece
        self.at_counts = self.at_links + self.packed
        self.payload = self.at_counts + self.units * self.row_hosts


def gather_kernel(s, tiles_ref, links_ref, hosts_ref, dangling_ref, local_ref, teleport_ref, out_ref):
    row, column = lax.axis_index("row"), lax.axis_index("col")
    counts = [[] for _ in range(s.units)]
    for a in range(s.tile_rows):
        tile_row = row * s.tile_rows + a
        first = tile_row * s.unit_hosts
        member = members(hosts_ref[pl.ds(tile_row, 1), :], first, s.unit_hosts)
        sums = mm(member.astype(bf16), links_ref[a * s.tile : (a + 1) * s.tile, :])
        for b in range(s.units):
            unit = column * s.units + b
            target = hosts_ref[pl.ds(unit, 1), :]
            valid = ~members(target, first, s.unit_hosts) & (dangling_ref[pl.ds(unit, 1), :] == 0)
            stored = (tiles_ref[a, b] > 0).astype(f32)
            part = sums[:, b * s.tile : (b + 1) * s.tile]
            counts[b].append(jnp.where(valid, part, 0.0) * stored)
    local = local_ref[...].astype(f32)
    half = s.piece // 2
    packed = jnp.concatenate([local[:half], local[half:]], axis=1).astype(bf16)
    values = jnp.concatenate(
        [teleport_ref[...].astype(bf16), packed]
        + [jnp.concatenate(c, axis=0).astype(bf16) for c in counts],
        axis=0,
    )
    for n in range(s.rows):
        out_ref[n] = values


def unpack_links(s, buffer_ref, first):
    parts = []
    low = iota((s.packed, LANES), 1) < s.piece
    for q in range(s.pair):
        packed = buffer_ref[first + q, s.at_links : s.at_counts, :].astype(f32)
        rolled = pltpu.roll(packed, s.piece, 1)
        parts += [jnp.where(low, packed, rolled), jnp.where(low, rolled, packed)]
    return jnp.concatenate(parts, axis=0)


def unpack_teleport(s, buffer_ref, first):
    return jnp.concatenate([buffer_ref[first + q, : s.piece, :] for q in range(s.pair)], axis=0)


def rank_kernel(s, buffer_ref, hosts_ref, dangling_ref, norm_ref, local_ref, aux_ref):
    column = lax.axis_index("col")
    ones = jnp.ones((s.tile, LANES), bf16)
    total = jnp.zeros((8, s.topics), f32)
    inverses, deads = [], []
    for m in range(s.units):
        unit = column * s.units + m
        hosts = hosts_ref[pl.ds(unit, 1), :]
        keep = (dangling_ref[pl.ds(unit, 1), :] == 0).astype(f32)
        member = members(hosts, unit * s.unit_hosts, s.unit_hosts).astype(f32)
        memberb = member.astype(bf16)
        same = mm_tn(memberb, memberb)
        sameb = same.astype(bf16)
        inside = unpack_links(s, buffer_ref, s.pair * m) * same * keep
        inward = jnp.sum(inside, axis=0, keepdims=True)
        size = jnp.sum(same, axis=0, keepdims=True)
        live = inward > 0
        step = inside * jnp.where(live, 1.0 / jnp.where(live, inward, 1.0), 0.0)
        step = step + same * jnp.where(live, 0.0, 1.0 / size)
        high, low = split(step)
        teleport = unpack_teleport(s, buffer_ref, s.pair * m)
        total = total + mm(ones[:8], teleport)
        restart = mm(sameb, ones) * teleport.astype(f32) / mm(sameb, teleport)
        ranks = damping * (mm(high, ones) + mm(low, ones)) + (1 - damping) * restart
        for _ in range(LOCAL_ITERS - 1):
            ranks_high, ranks_low = split(ranks)
            flow = mm(high, ranks_high) + mm(high, ranks_low) + mm(low, ranks_high)
            ranks = damping * flow + (1 - damping) * restart
        ranks_high, ranks_low = split(ranks)
        local_ref[m * s.tile : (m + 1) * s.tile, :] = ranks_high
        start = s.at_counts + m * s.row_hosts
        counts = jnp.concatenate(
            [buffer_ref[n, start : start + s.row_hosts, :] for n in range(s.rows)], axis=0
        )
        outward = mm(jnp.ones((8, s.hosts), bf16), counts)[:1]
        degree = inward + outward
        has_out = degree > 0
        inverse = jnp.where(has_out, 1.0 / jnp.where(has_out, degree, 1.0), 0.0)
        sums = mm_nt(ones[:8, : s.topics], ranks_high) + mm_nt(ones[:8, : s.topics], ranks_low)
        means = sums[:1] * (1.0 / s.topics) * inverse
        weights = mm_nt((member * means).astype(bf16), counts)
        out = jnp.sum(weights, axis=1, keepdims=True)
        linked = out > 0
        norm = jnp.where(linked, weights / jnp.where(linked, out, 1.0), 1.0 / s.hosts)
        norm_ref[m * s.unit_hosts : (m + 1) * s.unit_hosts, :] = norm
        inverses.append(inverse)
        deads.append(jnp.where(has_out, 0.0, 1.0 / s.pages))
    norm_ref[s.column_hosts :, : s.topics] = total
    aux_ref[...] = jnp.concatenate(inverses + deads, axis=0)


def edges_kernel(s, tiles_ref, links_ref, buffer_ref, hosts_ref, aux_ref, out_ref):
    row, column = lax.axis_index("row"), lax.axis_index("col")
    first = row * s.tile_rows - column * s.units
    for a in range(s.tile_rows):
        rows = slice(a * s.tile, (a + 1) * s.tile)
        for b in range(s.units):
            lanes = slice(b * s.tile, (b + 1) * s.tile)
            inverse = aux_ref[b : b + 1, :]
            dead = aux_ref[s.units + b : s.units + b + 1, :]
            scale = inverse * (tiles_ref[a, b] > 0).astype(f32)
            out_ref[rows, lanes] = links_ref[rows, lanes].astype(f32) * scale + dead

            @pl.when(first + a == b)
            def _():
                unit = column * s.units + b
                memberb = members(hosts_ref[pl.ds(unit, 1), :], unit * s.unit_hosts, s.unit_hosts)
                memberb = memberb.astype(bf16)
                same = mm_tn(memberb, memberb) > 0
                inside = unpack_links(s, buffer_ref, s.pair * b) * inverse
                across = links_ref[rows, lanes].astype(f32) * scale
                out_ref[rows, lanes] = jnp.where(same, inside, across) + dead


def flow_kernel(s, *refs):
    norms, (edges_ref, local_ref, buffer_ref, hosts_ref, out_ref, full_ref) = refs[: s.cols], refs[s.cols :]
    row, column = lax.axis_index("row"), lax.axis_index("col")
    total = jnp.zeros((8, s.topics), f32)
    for k in range(s.cols):
        at = pl.multiple_of((column ^ k) * s.column_hosts, s.column_hosts)
        full_ref[pl.ds(at, s.column_hosts), :] = norms[k][: s.column_hosts, :]
        total = total + norms[k][s.column_hosts :, : s.topics]
    norm = full_ref[...]
    norm_high, norm_low = split(norm)

    def three(x):
        high = x.astype(bf16).astype(f32)
        rest = x - high
        middle = rest.astype(bf16).astype(f32)
        where = iota((8, x.shape[1]), 0)
        parts = jnp.where(where == 0, high, jnp.where(where == 1, middle, rest - middle))
        return jnp.where(where < 3, parts, 0.0).astype(bf16)

    rank = damping * jnp.sum(norm, axis=0, keepdims=True) + (1 - damping)
    for _ in range(HOST_ITERS - 1):
        parts = three(rank)
        fresh = mm(parts, norm_high) + mm(parts, norm_low)
        rank = damping * jnp.sum(fresh, axis=0, keepdims=True) + (1 - damping)
    parts = three(rank)
    scales = []
    for b in range(s.units):
        hosts = hosts_ref[pl.ds(column * s.units + b, 1), :]
        chosen = mm(parts, members(hosts, 0, s.hosts).astype(bf16))
        scales.append(jnp.sum(chosen, axis=0, keepdims=True))
    scale = jnp.concatenate(scales, axis=1)
    tele_scale = (1 - damping) * s.pages / total[:1]
    first = row * s.cols - column * s.rows
    diagonal = (first >= 0) & (first < s.rows)
    for place, k in enumerate(exchange_order(s.cols)):
        chunk = column ^ k
        at = pl.multiple_of(chunk * s.piece, s.piece)
        weighted = (edges_ref[pl.ds(at, s.piece), :] * scale).astype(bf16)
        flow = damping * mm(weighted, local_ref[...])
        out_ref[place * s.piece : (place + 1) * s.piece, :] = flow

        @pl.when(diagonal)
        def _():
            own = buffer_ref[first + chunk, : s.piece, :].astype(f32) * tele_scale
            out_ref[place * s.piece : (place + 1) * s.piece, :] = flow + own


def exchange_order(count):
    bits = count.bit_length() - 1
    return [int(format(i, f"0{bits}b")[::-1], 2) if bits else 0 for i in range(count)]


def swap(x, count, bit):
    return lax.ppermute(x, "col", [(i, i ^ bit) for i in range(count)])


def on_device(links, tiles, local_links, host_ids, dangling, teleport):
    rows, cols = lax.axis_size("row"), lax.axis_size("col")
    pages = host_ids.shape[0]
    s = Sizes(rows, cols, links.shape, tiles.shape, local_links.shape, teleport.shape, pages)
    hosts = host_ids.reshape(pages // LANES, LANES)
    ignored = dangling.reshape(pages // LANES, LANES)
    sent = pl.pallas_call(
        functools.partial(gather_kernel, s),
        out_shape=jax.ShapeDtypeStruct((rows, s.payload, LANES), bf16),
        in_specs=[SMEM] + [VMEM] * 5,
        out_specs=VMEM,
    )(tiles, links, hosts, ignored, local_links, teleport)
    held = lax.all_to_all(sent, "row", 0, 0, tiled=True)
    norm, local, aux = pl.pallas_call(
        functools.partial(rank_kernel, s),
        out_shape=(
            jax.ShapeDtypeStruct((s.column_hosts + 8, s.hosts), f32),
            jax.ShapeDtypeStruct((s.width, s.topics), bf16),
            jax.ShapeDtypeStruct((2 * s.units, LANES), f32),
        ),
        in_specs=[VMEM] * 3,
        out_specs=(VMEM,) * 3,
    )(held, hosts, ignored)
    norms = {0: norm}
    bit = cols // 2
    while bit:
        norms.update({k ^ bit: swap(v, cols, bit) for k, v in norms.items()})
        bit //= 2
    edges = pl.pallas_call(
        functools.partial(edges_kernel, s),
        out_shape=jax.ShapeDtypeStruct((s.height, s.width), f32),
        in_specs=[SMEM] + [VMEM] * 4,
        out_specs=VMEM,
        cost_estimate=pl.CostEstimate(flops=10**6, bytes_accessed=10**6, transcendentals=0),
    )(tiles, links, held, hosts, aux)
    flows = pl.pallas_call(
        functools.partial(flow_kernel, s),
        out_shape=jax.ShapeDtypeStruct((s.height, s.topics), f32),
        in_specs=[VMEM] * (cols + 4),
        out_specs=VMEM,
        scratch_shapes=[pltpu.VMEM((s.hosts, s.hosts), f32)],
    )(*(norms[k] for k in range(cols)), edges, local, held, hosts)
    bit = 1
    while bit < cols:
        half = flows.shape[0] // 2
        flows = flows[:half] + swap(flows[half:], cols, bit)
        bit *= 2
    return flows


def solution(mesh):
    return jax.shard_map(
        on_device,
        mesh=mesh,
        in_specs=(
            P("row", "col"),
            P("row", "col"),
            P(("col", "row"), None),
            P(),
            P(),
            P(("col", "row"), None),
        ),
        out_specs=P(("row", "col"), None),
        check_vma=False,
    )
```

```python
import functools

import jax
import jax.numpy as jnp
from jax import lax
from jax.experimental import pallas as pl
from jax.experimental.pallas import tpu as pltpu
from jax.sharding import PartitionSpec as P


HOSTS_PIECE = 4
LOCAL_ITERS = 2
HOST_ITERS = 3
LANES = 128
GRANT = 24 * 2**20

damping = 0.85
f32 = jnp.float32
bf16 = jnp.bfloat16

VMEM = pl.BlockSpec(memory_space=pltpu.VMEM)
SMEM = pl.BlockSpec(memory_space=pltpu.SMEM)
HBM = pl.BlockSpec(memory_space=pltpu.HBM)


def iota(shape, axis):
    return lax.broadcasted_iota(jnp.int32, shape, axis)


def mm(a, b):
    return jnp.dot(a, b, preferred_element_type=f32)


def mm_nt(a, b):
    return lax.dot_general(a, b, (((1,), (1,)), ((), ())), preferred_element_type=f32)


def mm_tn(a, b):
    return lax.dot_general(a, b, (((0,), (0,)), ((), ())), preferred_element_type=f32)


def split(x):
    high = x.astype(bf16)
    return high, (x - high.astype(f32)).astype(bf16)


def members(hosts_row, first, count):
    return hosts_row == first + iota((count, hosts_row.shape[1]), 0)


class Sizes:
    def __init__(self, rows, cols, links, tiles, local_links, teleport, pages):
        self.rows, self.cols, self.pages = rows, cols, pages
        self.height, self.width = links
        self.piece = local_links[0]
        self.topics = teleport[1]
        self.tile = self.height // tiles[0]
        self.tile_rows, self.units = tiles
        self.pair = self.tile // self.piece
        self.unit_hosts = self.pair * HOSTS_PIECE
        self.hosts = HOSTS_PIECE * rows * cols
        self.column_hosts = HOSTS_PIECE * rows
        self.row_hosts = HOSTS_PIECE * cols
        self.packed = self.piece * self.piece // LANES
        self.at_counts = self.piece
        self.at_extra = self.at_counts + self.units * self.row_hosts
        self.payload = self.at_extra + 8
        self.extra = (self.units + 1 + 7) // 8 * 8


def rows_of(row, half, piece):
    rolled = pltpu.roll(row, piece, 1)
    low = iota(row.shape, 1) < piece
    first = jnp.where(low, row, rolled)
    second = jnp.where(low, rolled, row)
    return jnp.where(half == 0, first, second)


def first_kernel(s, tiles_hbm, links_hbm, hosts_hbm, dangling_hbm, local_hbm, teleport_hbm, *refs):
    sent_ref, own_ref, chunk_refs = refs[0], refs[1], refs[2 : 2 + s.cols]
    tiles_ref, links_ref, hosts_ref, dangling_ref, local_ref, teleport_ref, sem = refs[2 + s.cols :]
    copies = [
        pltpu.make_async_copy(source, target, sem.at[i])
        for i, (source, target) in enumerate(
            (
                (hosts_hbm, hosts_ref),
                (dangling_hbm, dangling_ref),
                (local_hbm, local_ref),
                (teleport_hbm, teleport_ref),
                (links_hbm, links_ref),
                (tiles_hbm, tiles_ref),
            )
        )
    ]
    for copy in copies:
        copy.start()
    row, column = lax.axis_index("row"), lax.axis_index("col")
    for copy in copies[:4]:
        copy.wait()
    piece = column * s.rows + row
    unit, half = piece // s.pair, piece % s.pair
    hosts = rows_of(hosts_ref[pl.ds(unit, 1), :], half, s.piece)[:, : s.piece]
    keep = rows_of(dangling_ref[pl.ds(unit, 1), :], half, s.piece)[:, : s.piece] == 0
    member = members(hosts, piece * HOSTS_PIECE, 8).astype(bf16)
    same = mm_tn(member, member)
    sameb = same.astype(bf16)
    local = local_ref[...].astype(f32)
    inside = local * same * keep.astype(f32)
    inward = jnp.sum(inside, axis=0, keepdims=True)
    size = jnp.sum(same, axis=0, keepdims=True)
    live = inward > 0
    step = inside * jnp.where(live, 1.0 / jnp.where(live, inward, 1.0), 0.0)
    step = step + same * jnp.where(live, 0.0, 1.0 / size)
    high, low = split(step)
    teleport = teleport_ref[...]
    tele_high, tele_low = split(teleport)
    sizes = jnp.sum(same, axis=1, keepdims=True)
    restart = sizes * teleport / (mm(sameb, tele_high) + mm(sameb, tele_low))
    ranks = damping * jnp.sum(step, axis=1, keepdims=True) + (1 - damping) * restart
    for _ in range(LOCAL_ITERS - 1):
        ranks_high, ranks_low = split(ranks)
        flow = mm(high, ranks_high) + mm(high, ranks_low) + mm(low, ranks_high)
        ranks = damping * flow + (1 - damping) * restart
    half_piece = s.piece // 2
    packed = jnp.concatenate([local[:half_piece], local[half_piece:]], axis=1).astype(bf16)
    own_ref[: s.piece, :] = tele_high
    own_ref[s.piece :, :] = packed
    total = jnp.sum(teleport, axis=0, keepdims=True)
    total_high = total.astype(bf16).astype(f32)
    where = iota((8, LANES), 0)
    inward = jnp.concatenate([inward, inward], axis=1)
    extra = jnp.where(where == 0, inward, jnp.where(where == 1, total_high, total - total_high))

    for copy in copies[4:]:
        copy.wait()
    counts = [[] for _ in range(s.units)]
    for a in range(s.tile_rows):
        tile_row = row * s.tile_rows + a
        first = tile_row * s.unit_hosts
        member = members(hosts_ref[pl.ds(tile_row, 1), :], first, s.unit_hosts)
        sums = mm(member.astype(bf16), links_ref[a * s.tile : (a + 1) * s.tile, :])
        for b in range(s.units):
            unit = column * s.units + b
            target = hosts_ref[pl.ds(unit, 1), :]
            valid = ~members(target, first, s.unit_hosts) & (dangling_ref[pl.ds(unit, 1), :] == 0)
            stored = (tiles_ref[a, b] > 0).astype(f32)
            part = sums[:, b * s.tile : (b + 1) * s.tile]
            counts[b].append(jnp.where(valid, part, 0.0) * stored)
    for k in range(s.cols):
        chunk = column ^ k
        at = pl.multiple_of(chunk * s.piece, s.piece)
        for b in range(s.units):
            lanes = slice(b * s.tile, (b + 1) * s.tile)
            stored = (tiles_ref[chunk // s.pair, b] > 0).astype(f32).astype(bf16)
            chunk_refs[k][:, lanes] = links_ref[pl.ds(at, s.piece), lanes] * stored
    values = jnp.concatenate(
        [ranks.astype(bf16)]
        + [jnp.concatenate(c, axis=0).astype(bf16) for c in counts]
        + [extra.astype(bf16)],
        axis=0,
    )
    for n in range(s.rows):
        sent_ref[n] = values


def graph_kernel(s, buffer_ref, hosts_ref, shared_ref, local_ref):
    column = lax.axis_index("col")
    ones = jnp.ones((8, LANES), bf16)
    low = iota((1, LANES), 1) < s.piece
    extras = [buffer_ref[n, s.at_extra :, :].astype(f32) for n in range(s.rows)]
    total = functools.reduce(jnp.add, [e[1:2] + e[2:3] for e in extras])
    for m in range(s.units):
        unit = column * s.units + m
        member = members(hosts_ref[pl.ds(unit, 1), :], unit * s.unit_hosts, s.unit_hosts)
        start = s.at_counts + m * s.row_hosts
        counts = jnp.concatenate(
            [buffer_ref[n, start : start + s.row_hosts, :] for n in range(s.rows)], axis=0
        )
        ranks = jnp.concatenate(
            [buffer_ref[s.pair * m + q, : s.piece, :] for q in range(s.pair)], axis=0
        )
        local_ref[m * s.tile : (m + 1) * s.tile, :] = ranks
        inward = jnp.where(low, extras[s.pair * m][:1], extras[s.pair * m + 1][:1])
        degree = inward + mm(jnp.ones((8, s.hosts), bf16), counts)[:1]
        has_out = degree > 0
        inverse = jnp.where(has_out, 1.0 / jnp.where(has_out, degree, 1.0), 0.0)
        means = mm_nt(ones[:, : s.topics], ranks)[:1] * (1.0 / s.topics) * inverse
        weights = mm_nt((member.astype(f32) * means).astype(bf16), counts)
        out = jnp.sum(weights, axis=1, keepdims=True)
        linked = out > 0
        norm = jnp.where(linked, weights / jnp.where(linked, out, 1.0), 1.0 / s.hosts)
        shared_ref[m * s.unit_hosts : (m + 1) * s.unit_hosts, :] = norm
        shared_ref[s.column_hosts + m : s.column_hosts + m + 1, :LANES] = inverse
    shared_ref[s.column_hosts + s.units : s.column_hosts + s.units + 1, : s.topics] = total


def edges_kernel(s, own_ref, hosts_ref, dangling_ref, *refs):
    chunk_refs, out_ref = refs[: s.cols], refs[s.cols]
    row, column = lax.axis_index("row"), lax.axis_index("col")
    for k in range(s.cols):
        at = pl.multiple_of((column ^ k) * s.width, s.width)
        out_ref[:, pl.ds(at, s.width)] = chunk_refs[k][...]
    piece = row * s.cols + column
    unit, half = piece // s.pair, piece % s.pair
    hosts = hosts_ref[pl.ds(unit, 1), :]
    keep = dangling_ref[pl.ds(unit, 1), :] == 0
    mine = rows_of(hosts, half, s.piece)[:, : s.piece]
    first = piece * HOSTS_PIECE
    same = mm_tn(members(mine, first, 8).astype(bf16), members(hosts, first, 8).astype(bf16)) > 0
    packed = own_ref[s.piece :, :].astype(f32)
    rolled = pltpu.roll(packed, s.piece, 1)
    low = iota((s.packed, LANES), 1) < s.piece
    local = jnp.concatenate([jnp.where(low, packed, rolled), jnp.where(low, rolled, packed)], axis=0)
    at = pl.multiple_of(unit * s.tile, s.tile)
    across = out_ref[:, pl.ds(at, s.tile)].astype(f32)
    fixed = jnp.where(same, jnp.where(keep, local, 0.0), across)
    out_ref[:, pl.ds(at, s.tile)] = fixed.astype(bf16)


def three(x):
    high = x.astype(bf16).astype(f32)
    rest = x - high
    middle = rest.astype(bf16).astype(f32)
    where = iota((8, x.shape[1]), 0)
    parts = jnp.where(where == 0, high, jnp.where(where == 1, middle, rest - middle))
    return jnp.where(where < 3, parts, 0.0).astype(bf16)


def host_kernel(s, own_ref, hosts_ref, edges_ref, *refs):
    shared, (weighted_ref, base_ref, full_ref, inverse_ref) = refs[: s.cols], refs[s.cols :]
    column = lax.axis_index("col")
    total = jnp.zeros((1, s.topics), f32)
    for k in range(s.cols):
        at = pl.multiple_of((column ^ k) * s.column_hosts, s.column_hosts)
        full_ref[pl.ds(at, s.column_hosts), :] = shared[k][: s.column_hosts, :]
        end = s.column_hosts + s.units
        inverse_ref[pl.ds((column ^ k) * s.units, s.units), :] = shared[k][s.column_hosts : end, :LANES]
        total = total + shared[k][end : end + 1, : s.topics]
    base_ref[...] = (1 - damping) * s.pages * own_ref[: s.piece, :].astype(f32) / total
    norm = full_ref[...]
    norm_high, norm_low = split(norm)
    rank = damping * jnp.sum(norm, axis=0, keepdims=True) + (1 - damping)
    for _ in range(HOST_ITERS - 1):
        parts = three(rank)
        fresh = mm(parts, norm_high) + mm(parts, norm_low)
        rank = damping * jnp.sum(fresh, axis=0, keepdims=True) + (1 - damping)
    block = LANES // s.unit_hosts
    all_units = s.units * s.cols
    for g in range(s.hosts // LANES):
        count = min(block, all_units - g * block)
        hosts = hosts_ref[g * block : g * block + count, :] - g * LANES
        ranks = jnp.broadcast_to(rank[:, g * LANES : (g + 1) * LANES], (count, LANES))
        page = damping * jnp.take_along_axis(ranks, hosts, axis=1)
        inverse = inverse_ref[g * block : g * block + count, :]
        scale = page * inverse
        dead = jnp.where(inverse > 0, 0.0, page * (1.0 / s.pages))
        for u in range(count):
            at = (g * block + u) * s.tile
            lanes = slice(at, at + s.tile)
            links = edges_ref[:, lanes].astype(f32)
            weighted_ref[:, lanes] = (links * scale[u : u + 1] + dead[u : u + 1]).astype(bf16)


def flow_kernel(s, weighted_ref, base_ref, *refs):
    locals_, out_ref = refs[: s.cols], refs[s.cols]
    column = lax.axis_index("col")
    flow = base_ref[...]
    for k in range(s.cols):
        at = pl.multiple_of((column ^ k) * s.width, s.width)
        flow = flow + mm(weighted_ref[:, pl.ds(at, s.width)], locals_[k][...])
    out_ref[...] = flow


def in_hbm(x):
    return pltpu.with_memory_space_constraint(x, pltpu.HBM)


def swap(x, count, bits):
    return lax.ppermute(x, "col", [(i, i ^ bits) for i in range(count)])


def gathered(x, count):
    found = {0: x}
    bit = count // 2
    while bit:
        for k, v in list(found.items()):
            found[k ^ bit] = swap(v, count, bit)
        bit //= 2
    return [found[k] for k in range(count)]


def call(kernel, out_shape, in_specs, scratch=(), cost=10**6):
    single = not isinstance(out_shape, tuple)
    return pl.pallas_call(
        kernel,
        out_shape=out_shape,
        in_specs=in_specs,
        out_specs=VMEM if single else (VMEM,) * len(out_shape),
        scratch_shapes=scratch,
        compiler_params=pltpu.CompilerParams(vmem_limit_bytes=GRANT),
        cost_estimate=pl.CostEstimate(flops=cost, bytes_accessed=cost, transcendentals=0),
    )


def on_device(links, tiles, local_links, host_ids, dangling, teleport):
    rows, cols = lax.axis_size("row"), lax.axis_size("col")
    pages = host_ids.shape[0]
    s = Sizes(rows, cols, links.shape, tiles.shape, local_links.shape, teleport.shape, pages)
    hosts = host_ids.reshape(pages // LANES, LANES)
    ignored = dangling.reshape(pages // LANES, LANES)
    shape = jax.ShapeDtypeStruct
    sent, own, *chunks = call(
        functools.partial(first_kernel, s),
        (
            shape((rows, s.payload, LANES), bf16),
            shape((s.piece + s.packed, LANES), bf16),
            *(shape((s.piece, s.width), bf16) for _ in range(cols)),
        ),
        [HBM] * 6,
        [pltpu.SMEM(tiles.shape, tiles.dtype)]
        + [pltpu.VMEM(a.shape, a.dtype) for a in (links, hosts, ignored, local_links, teleport)]
        + [pltpu.SemaphoreType.DMA((6,))],
    )(*(in_hbm(x) for x in (tiles, links, hosts, ignored, local_links, teleport)))
    moves = [(r * cols + c, c * rows + r) for r in range(rows) for c in range(cols)]
    own = lax.ppermute(own, ("row", "col"), moves)
    for k in range(1, cols):
        chunks[k] = swap(chunks[k], cols, k)
    held = lax.all_to_all(sent, "row", 0, 0, tiled=True)
    shared, local = call(
        functools.partial(graph_kernel, s),
        (
            shape((s.column_hosts + s.extra, s.hosts), f32),
            shape((s.width, s.topics), bf16),
        ),
        [VMEM] * 2,
    )(held, hosts)
    shared = gathered(shared, cols)
    locals_ = gathered(local, cols)
    edges = call(
        functools.partial(edges_kernel, s),
        shape((s.piece, pages), bf16),
        [VMEM] * (3 + cols),
    )(own, hosts, ignored, *chunks)
    weighted, base = call(
        functools.partial(host_kernel, s),
        (shape((s.piece, pages), bf16), shape((s.piece, s.topics), f32)),
        [VMEM] * (3 + cols),
        [pltpu.VMEM((s.hosts, s.hosts), f32), pltpu.VMEM((s.units * cols, LANES), f32)],
    )(own, hosts, edges, *shared)
    return call(
        functools.partial(flow_kernel, s),
        shape((s.piece, s.topics), f32),
        [VMEM] * (2 + cols),
    )(weighted, base, *locals_)


def solution(mesh):
    return jax.shard_map(
        on_device,
        mesh=mesh,
        in_specs=(
            P("row", "col"),
            P("row", "col"),
            P(("col", "row"), None),
            P(),
            P(),
            P(("col", "row"), None),
        ),
        out_specs=P(("row", "col"), None),
        check_vma=False,
    )
```

```python
import functools

import jax
import jax.numpy as jnp
from jax import lax
from jax.experimental import pallas as pl
from jax.experimental.pallas import tpu as pltpu
from jax.sharding import PartitionSpec as P


HOSTS_PIECE = 4
LOCAL_ITERS = 2
HOST_ITERS = 3
LANES = 128
GRANT = 24 * 2**20

damping = 0.85
f32 = jnp.float32
bf16 = jnp.bfloat16

VMEM = pl.BlockSpec(memory_space=pltpu.VMEM)
SMEM = pl.BlockSpec(memory_space=pltpu.SMEM)
HBM = pl.BlockSpec(memory_space=pltpu.HBM)


def iota(shape, axis):
    return lax.broadcasted_iota(jnp.int32, shape, axis)


def mm(a, b):
    return jnp.dot(a, b, preferred_element_type=f32)


def mm_nt(a, b):
    return lax.dot_general(a, b, (((1,), (1,)), ((), ())), preferred_element_type=f32)


def mm_tn(a, b):
    return lax.dot_general(a, b, (((0,), (0,)), ((), ())), preferred_element_type=f32)


def split(x):
    high = x.astype(bf16)
    return high, (x - high.astype(f32)).astype(bf16)


def members(hosts_row, first, count):
    return hosts_row == first + iota((count, hosts_row.shape[1]), 0)


class Sizes:
    def __init__(self, rows, cols, links, tiles, local_links, teleport, pages):
        self.rows, self.cols, self.pages = rows, cols, pages
        self.height, self.width = links
        self.piece = local_links[0]
        self.topics = teleport[1]
        self.tile = self.height // tiles[0]
        self.tile_rows, self.units = tiles
        self.pair = self.tile // self.piece
        self.unit_hosts = self.pair * HOSTS_PIECE
        self.hosts = HOSTS_PIECE * rows * cols
        self.column_hosts = HOSTS_PIECE * rows
        self.row_hosts = HOSTS_PIECE * cols
        self.packed = self.piece * self.piece // LANES
        self.at_counts = self.piece
        self.at_extra = self.at_counts + self.units * self.row_hosts
        self.payload = self.at_extra + 8
        self.extra = (self.units + 1 + 7) // 8 * 8


def rows_of(row, half, piece):
    rolled = pltpu.roll(row, piece, 1)
    low = iota(row.shape, 1) < piece
    first = jnp.where(low, row, rolled)
    second = jnp.where(low, rolled, row)
    return jnp.where(half == 0, first, second)


def first_kernel(s, tiles_hbm, links_hbm, hosts_hbm, dangling_hbm, local_hbm, teleport_hbm, *refs):
    sent_ref, own_ref, chunk_refs = refs[0], refs[1], refs[2 : 2 + s.cols]
    tiles_ref, links_ref, hosts_ref, dangling_ref, local_ref, teleport_ref, sem = refs[2 + s.cols :]
    copies = [
        pltpu.make_async_copy(source, target, sem.at[i])
        for i, (source, target) in enumerate(
            (
                (hosts_hbm, hosts_ref),
                (dangling_hbm, dangling_ref),
                (local_hbm, local_ref),
                (teleport_hbm, teleport_ref),
                (links_hbm, links_ref),
                (tiles_hbm, tiles_ref),
            )
        )
    ]
    for copy in copies:
        copy.start()
    row, column = lax.axis_index("row"), lax.axis_index("col")
    for copy in copies[:4]:
        copy.wait()
    piece = column * s.rows + row
    unit, half = piece // s.pair, piece % s.pair
    hosts = rows_of(hosts_ref[pl.ds(unit, 1), :], half, s.piece)[:, : s.piece]
    keep = rows_of(dangling_ref[pl.ds(unit, 1), :], half, s.piece)[:, : s.piece] == 0
    member = members(hosts, piece * HOSTS_PIECE, 8).astype(bf16)
    same = mm_tn(member, member)
    sameb = same.astype(bf16)
    local = local_ref[...].astype(f32)
    inside = local * same * keep.astype(f32)
    inward = jnp.sum(inside, axis=0, keepdims=True)
    size = jnp.sum(same, axis=0, keepdims=True)
    live = inward > 0
    step = inside * jnp.where(live, 1.0 / jnp.where(live, inward, 1.0), 0.0)
    step = step + same * jnp.where(live, 0.0, 1.0 / size)
    high, low = split(step)
    teleport = teleport_ref[...]
    tele_high, tele_low = split(teleport)
    sizes = jnp.sum(same, axis=1, keepdims=True)
    restart = sizes * teleport / (mm(sameb, tele_high) + mm(sameb, tele_low))
    ranks = damping * jnp.sum(step, axis=1, keepdims=True) + (1 - damping) * restart
    for _ in range(LOCAL_ITERS - 1):
        ranks_high, ranks_low = split(ranks)
        flow = mm(high, ranks_high) + mm(high, ranks_low) + mm(low, ranks_high)
        ranks = damping * flow + (1 - damping) * restart
    half_piece = s.piece // 2
    packed = jnp.concatenate([local[:half_piece], local[half_piece:]], axis=1).astype(bf16)
    own_ref[: s.piece, :] = tele_high
    own_ref[s.piece :, :] = packed
    total = jnp.sum(teleport, axis=0, keepdims=True)
    total_high = total.astype(bf16).astype(f32)
    where = iota((8, LANES), 0)
    inward = jnp.concatenate([inward, inward], axis=1)
    extra = jnp.where(where == 0, inward, jnp.where(where == 1, total_high, total - total_high))

    for copy in copies[4:]:
        copy.wait()
    counts = [[] for _ in range(s.units)]
    for a in range(s.tile_rows):
        tile_row = row * s.tile_rows + a
        first = tile_row * s.unit_hosts
        member = members(hosts_ref[pl.ds(tile_row, 1), :], first, s.unit_hosts)
        sums = mm(member.astype(bf16), links_ref[a * s.tile : (a + 1) * s.tile, :])
        for b in range(s.units):
            unit = column * s.units + b
            target = hosts_ref[pl.ds(unit, 1), :]
            valid = ~members(target, first, s.unit_hosts) & (dangling_ref[pl.ds(unit, 1), :] == 0)
            stored = (tiles_ref[a, b] > 0).astype(f32)
            part = sums[:, b * s.tile : (b + 1) * s.tile]
            counts[b].append(jnp.where(valid, part, 0.0) * stored)
    for k in range(s.cols):
        chunk = column ^ k
        at = pl.multiple_of(chunk * s.piece, s.piece)
        for b in range(s.units):
            lanes = slice(b * s.tile, (b + 1) * s.tile)
            stored = (tiles_ref[chunk // s.pair, b] > 0).astype(f32).astype(bf16)
            chunk_refs[k][:, lanes] = links_ref[pl.ds(at, s.piece), lanes] * stored
    values = jnp.concatenate(
        [ranks.astype(bf16)]
        + [jnp.concatenate(c, axis=0).astype(bf16) for c in counts]
        + [extra.astype(bf16)],
        axis=0,
    )
    for n in range(s.rows):
        sent_ref[n] = values


def ranks_kernel(s, buffer_ref, local_ref):
    for n in range(s.rows):
        local_ref[n * s.piece : (n + 1) * s.piece, :] = buffer_ref[n, : s.piece, :]


def graph_kernel(s, buffer_ref, hosts_ref, local_ref, shared_ref):
    column = lax.axis_index("col")
    ones = jnp.ones((8, LANES), bf16)
    low = iota((1, LANES), 1) < s.piece
    extras = [buffer_ref[n, s.at_extra :, :].astype(f32) for n in range(s.rows)]
    total = functools.reduce(jnp.add, [e[1:2] + e[2:3] for e in extras])
    for m in range(s.units):
        unit = column * s.units + m
        member = members(hosts_ref[pl.ds(unit, 1), :], unit * s.unit_hosts, s.unit_hosts)
        start = s.at_counts + m * s.row_hosts
        counts = jnp.concatenate(
            [buffer_ref[n, start : start + s.row_hosts, :] for n in range(s.rows)], axis=0
        )
        ranks = local_ref[m * s.tile : (m + 1) * s.tile, :]
        inward = jnp.where(low, extras[s.pair * m][:1], extras[s.pair * m + 1][:1])
        degree = inward + mm(jnp.ones((8, s.hosts), bf16), counts)[:1]
        has_out = degree > 0
        inverse = jnp.where(has_out, 1.0 / jnp.where(has_out, degree, 1.0), 0.0)
        means = mm_nt(ones[:, : s.topics], ranks)[:1] * (1.0 / s.topics) * inverse
        weights = mm_nt((member.astype(f32) * means).astype(bf16), counts)
        out = jnp.sum(weights, axis=1, keepdims=True)
        linked = out > 0
        norm = jnp.where(linked, weights / jnp.where(linked, out, 1.0), 1.0 / s.hosts)
        shared_ref[m * s.unit_hosts : (m + 1) * s.unit_hosts, :] = norm
        shared_ref[s.column_hosts + m : s.column_hosts + m + 1, :LANES] = inverse
    shared_ref[s.column_hosts + s.units : s.column_hosts + s.units + 1, : s.topics] = total


def edges_kernel(s, own_ref, hosts_ref, dangling_ref, *refs):
    chunk_refs, out_ref = refs[: s.cols], refs[s.cols]
    row, column = lax.axis_index("row"), lax.axis_index("col")
    for k in range(s.cols):
        at = pl.multiple_of((column ^ k) * s.width, s.width)
        out_ref[:, pl.ds(at, s.width)] = chunk_refs[k][...]
    piece = row * s.cols + column
    unit, half = piece // s.pair, piece % s.pair
    hosts = hosts_ref[pl.ds(unit, 1), :]
    keep = dangling_ref[pl.ds(unit, 1), :] == 0
    mine = rows_of(hosts, half, s.piece)[:, : s.piece]
    first = piece * HOSTS_PIECE
    same = mm_tn(members(mine, first, 8).astype(bf16), members(hosts, first, 8).astype(bf16)) > 0
    packed = own_ref[s.piece :, :].astype(f32)
    rolled = pltpu.roll(packed, s.piece, 1)
    low = iota((s.packed, LANES), 1) < s.piece
    local = jnp.concatenate([jnp.where(low, packed, rolled), jnp.where(low, rolled, packed)], axis=0)
    at = pl.multiple_of(unit * s.tile, s.tile)
    across = out_ref[:, pl.ds(at, s.tile)].astype(f32)
    fixed = jnp.where(same, jnp.where(keep, local, 0.0), across)
    out_ref[:, pl.ds(at, s.tile)] = fixed.astype(bf16)


def three(x):
    high = x.astype(bf16).astype(f32)
    rest = x - high
    middle = rest.astype(bf16).astype(f32)
    where = iota((8, x.shape[1]), 0)
    parts = jnp.where(where == 0, high, jnp.where(where == 1, middle, rest - middle))
    return jnp.where(where < 3, parts, 0.0).astype(bf16)


def host_kernel(s, own_ref, hosts_ref, edges_ref, *refs):
    shared, (weighted_ref, base_ref, full_ref, inverse_ref) = refs[: s.cols], refs[s.cols :]
    column = lax.axis_index("col")
    total = jnp.zeros((1, s.topics), f32)
    for k in range(s.cols):
        at = pl.multiple_of((column ^ k) * s.column_hosts, s.column_hosts)
        full_ref[pl.ds(at, s.column_hosts), :] = shared[k][: s.column_hosts, :]
        end = s.column_hosts + s.units
        inverse_ref[pl.ds((column ^ k) * s.units, s.units), :] = shared[k][s.column_hosts : end, :LANES]
        total = total + shared[k][end : end + 1, : s.topics]
    base_ref[...] = (1 - damping) * s.pages * own_ref[: s.piece, :].astype(f32) / total
    norm = full_ref[...]
    norm_high, norm_low = split(norm)
    rank = damping * jnp.sum(norm, axis=0, keepdims=True) + (1 - damping)
    for _ in range(HOST_ITERS - 1):
        parts = three(rank)
        fresh = mm(parts, norm_high) + mm(parts, norm_low)
        rank = damping * jnp.sum(fresh, axis=0, keepdims=True) + (1 - damping)
    block = LANES // s.unit_hosts
    all_units = s.units * s.cols
    for g in range(s.hosts // LANES):
        count = min(block, all_units - g * block)
        hosts = hosts_ref[g * block : g * block + count, :] - g * LANES
        ranks = jnp.broadcast_to(rank[:, g * LANES : (g + 1) * LANES], (count, LANES))
        page = damping * jnp.take_along_axis(ranks, hosts, axis=1)
        inverse = inverse_ref[g * block : g * block + count, :]
        scale = page * inverse
        dead = jnp.where(inverse > 0, 0.0, page * (1.0 / s.pages))
        for u in range(count):
            at = (g * block + u) * s.tile
            lanes = slice(at, at + s.tile)
            links = edges_ref[:, lanes].astype(f32)
            weighted_ref[:, lanes] = (links * scale[u : u + 1] + dead[u : u + 1]).astype(bf16)


def flow_kernel(s, distances, weighted_ref, base_ref, *refs):
    locals_, out_ref = refs[:-1], refs[-1]
    column = lax.axis_index("col")
    flow = base_ref[...]
    for k, local_ref in zip(distances, locals_, strict=True):
        at = pl.multiple_of((column ^ k) * s.width, s.width)
        flow = flow + mm(weighted_ref[:, pl.ds(at, s.width)], local_ref[...])
    out_ref[...] = flow


def in_hbm(x):
    return pltpu.with_memory_space_constraint(x, pltpu.HBM)


def swap(x, count, bits):
    return lax.ppermute(x, "col", [(i, i ^ bits) for i in range(count)])


def gathered(x, count):
    found = {0: x}
    bit = count // 2
    while bit:
        for k, v in list(found.items()):
            found[k ^ bit] = swap(v, count, bit)
        bit //= 2
    return [found[k] for k in range(count)]


def spread(values, count):
    found = [values[0]]
    for k in range(1, count):
        found.append(swap(values[k], count, k))
    return found


def call(kernel, out_shape, in_specs, scratch=(), cost=10**6):
    single = not isinstance(out_shape, tuple)
    return pl.pallas_call(
        kernel,
        out_shape=out_shape,
        in_specs=in_specs,
        out_specs=VMEM if single else (VMEM,) * len(out_shape),
        scratch_shapes=scratch,
        compiler_params=pltpu.CompilerParams(vmem_limit_bytes=GRANT),
        cost_estimate=pl.CostEstimate(flops=cost, bytes_accessed=cost, transcendentals=0),
    )


def on_device(links, tiles, local_links, host_ids, dangling, teleport):
    rows, cols = lax.axis_size("row"), lax.axis_size("col")
    pages = host_ids.shape[0]
    s = Sizes(rows, cols, links.shape, tiles.shape, local_links.shape, teleport.shape, pages)
    hosts = host_ids.reshape(pages // LANES, LANES)
    ignored = dangling.reshape(pages // LANES, LANES)
    shape = jax.ShapeDtypeStruct
    sent, own, *chunks = call(
        functools.partial(first_kernel, s),
        (
            shape((rows, s.payload, LANES), bf16),
            shape((s.piece + s.packed, LANES), bf16),
            *(shape((s.piece, s.width), bf16) for _ in range(cols)),
        ),
        [HBM] * 6,
        [pltpu.SMEM(tiles.shape, tiles.dtype)]
        + [pltpu.VMEM(a.shape, a.dtype) for a in (links, hosts, ignored, local_links, teleport)]
        + [pltpu.SemaphoreType.DMA((6,))],
    )(*(in_hbm(x) for x in (tiles, links, hosts, ignored, local_links, teleport)))
    moves = [(r * cols + c, c * rows + r) for r in range(rows) for c in range(cols)]
    own = lax.ppermute(own, ("row", "col"), moves)
    chunks = spread(chunks, cols)
    held = lax.all_to_all(sent, "row", 0, 0, tiled=True)
    local = call(functools.partial(ranks_kernel, s), shape((s.width, s.topics), bf16), [VMEM])(held)
    locals_ = gathered(local, cols)
    shared = call(
        functools.partial(graph_kernel, s),
        shape((s.column_hosts + s.extra, s.hosts), f32),
        [VMEM] * 3,
    )(held, hosts, local)
    shared = spread([shared] * cols, cols)
    edges = call(
        functools.partial(edges_kernel, s),
        shape((s.piece, pages), bf16),
        [VMEM] * (3 + cols),
    )(own, hosts, ignored, *chunks)
    weighted, base = call(
        functools.partial(host_kernel, s),
        (shape((s.piece, pages), bf16), shape((s.piece, s.topics), f32)),
        [VMEM] * (3 + cols),
        [pltpu.VMEM((s.hosts, s.hosts), f32), pltpu.VMEM((s.units * cols, LANES), f32)],
    )(own, hosts, edges, *shared)
    late = [k for k in range(cols) if k % 2 and k > 1]
    soon = [k for k in range(cols) if k not in late]
    flow = base
    for distances in (soon, late):
        flow = call(
            functools.partial(flow_kernel, s, distances),
            shape((s.piece, s.topics), f32),
            [VMEM] * (2 + len(distances)),
        )(weighted, flow, *(locals_[k] for k in distances))
    return flow


def solution(mesh):
    return jax.shard_map(
        on_device,
        mesh=mesh,
        in_specs=(
            P("row", "col"),
            P("row", "col"),
            P(("col", "row"), None),
            P(),
            P(),
            P(("col", "row"), None),
        ),
        out_specs=P(("row", "col"), None),
        check_vma=False,
    )
```

```python
import functools

import jax
import jax.numpy as jnp
from jax import lax
from jax.experimental import pallas as pl
from jax.experimental.pallas import tpu as pltpu
from jax.sharding import PartitionSpec as P


HOSTS_PIECE = 4
LOCAL_ITERS = 2
HOST_ITERS = 3
LANES = 128
GRANT = 24 * 2**20

damping = 0.85
f32 = jnp.float32
bf16 = jnp.bfloat16

VMEM = pl.BlockSpec(memory_space=pltpu.VMEM)
SMEM = pl.BlockSpec(memory_space=pltpu.SMEM)
HBM = pl.BlockSpec(memory_space=pltpu.HBM)


def iota(shape, axis):
    return lax.broadcasted_iota(jnp.int32, shape, axis)


def mm(a, b):
    return jnp.dot(a, b, preferred_element_type=f32)


def mm_nt(a, b):
    return lax.dot_general(a, b, (((1,), (1,)), ((), ())), preferred_element_type=f32)


def mm_tn(a, b):
    return lax.dot_general(a, b, (((0,), (0,)), ((), ())), preferred_element_type=f32)


def split(x):
    high = x.astype(bf16)
    return high, (x - high.astype(f32)).astype(bf16)


def members(hosts_row, first, count):
    return hosts_row == first + iota((count, hosts_row.shape[1]), 0)


class Sizes:
    def __init__(self, rows, cols, links, tiles, local_links, teleport, pages):
        self.rows, self.cols, self.pages = rows, cols, pages
        self.height, self.width = links
        self.piece = local_links[0]
        self.topics = teleport[1]
        self.tile = self.height // tiles[0]
        self.tile_rows, self.units = tiles
        self.pair = self.tile // self.piece
        self.unit_hosts = self.pair * HOSTS_PIECE
        self.hosts = HOSTS_PIECE * rows * cols
        self.column_hosts = HOSTS_PIECE * rows
        self.row_hosts = HOSTS_PIECE * cols
        self.packed = self.piece * self.piece // LANES
        self.at_counts = self.piece
        self.at_extra = self.at_counts + self.units * self.row_hosts
        self.payload = self.at_extra + 8
        self.extra = (self.units + 1 + 7) // 8 * 8

    def row_at(self, place):
        return (place + self.rows // 2) % self.rows

    def place_of(self, row):
        return (row - self.rows // 2) % self.rows


def rows_of(row, half, piece):
    rolled = pltpu.roll(row, piece, 1)
    low = iota(row.shape, 1) < piece
    first = jnp.where(low, row, rolled)
    second = jnp.where(low, rolled, row)
    return jnp.where(half == 0, first, second)


def first_kernel(s, tiles_hbm, links_hbm, hosts_hbm, dangling_hbm, local_hbm, teleport_hbm, *refs):
    sent_ref, own_ref, chunk_refs = refs[0], refs[1], refs[2 : 2 + s.cols]
    tiles_ref, links_ref, hosts_ref, dangling_ref, local_ref, teleport_ref, sem = refs[2 + s.cols :]
    copies = [
        pltpu.make_async_copy(source, target, sem.at[i])
        for i, (source, target) in enumerate(
            (
                (hosts_hbm, hosts_ref),
                (dangling_hbm, dangling_ref),
                (local_hbm, local_ref),
                (teleport_hbm, teleport_ref),
                (links_hbm, links_ref),
                (tiles_hbm, tiles_ref),
            )
        )
    ]
    for copy in copies:
        copy.start()
    row, column = lax.axis_index("row"), lax.axis_index("col")
    for copy in copies[:4]:
        copy.wait()
    piece = column * s.rows + row
    unit, half = piece // s.pair, piece % s.pair
    hosts = rows_of(hosts_ref[pl.ds(unit, 1), :], half, s.piece)[:, : s.piece]
    keep = rows_of(dangling_ref[pl.ds(unit, 1), :], half, s.piece)[:, : s.piece] == 0
    member = members(hosts, piece * HOSTS_PIECE, 8).astype(bf16)
    same = mm_tn(member, member)
    sameb = same.astype(bf16)
    local = local_ref[...].astype(f32)
    inside = local * same * keep.astype(f32)
    inward = jnp.sum(inside, axis=0, keepdims=True)
    size = jnp.sum(same, axis=0, keepdims=True)
    live = inward > 0
    step = inside * jnp.where(live, 1.0 / jnp.where(live, inward, 1.0), 0.0)
    step = step + same * jnp.where(live, 0.0, 1.0 / size)
    high, low = split(step)
    teleport = teleport_ref[...]
    tele_high, tele_low = split(teleport)
    sizes = jnp.sum(same, axis=1, keepdims=True)
    restart = sizes * teleport / (mm(sameb, tele_high) + mm(sameb, tele_low))
    ranks = damping * jnp.sum(step, axis=1, keepdims=True) + (1 - damping) * restart
    for _ in range(LOCAL_ITERS - 1):
        ranks_high, ranks_low = split(ranks)
        flow = mm(high, ranks_high) + mm(high, ranks_low) + mm(low, ranks_high)
        ranks = damping * flow + (1 - damping) * restart
    half_piece = s.piece // 2
    packed = jnp.concatenate([local[:half_piece], local[half_piece:]], axis=1).astype(bf16)
    own_ref[: s.piece, :] = tele_high
    own_ref[s.piece :, :] = packed
    total = jnp.sum(teleport, axis=0, keepdims=True)
    total_high = total.astype(bf16).astype(f32)
    where = iota((8, LANES), 0)
    inward = jnp.concatenate([inward, inward], axis=1)
    extra = jnp.where(where == 0, inward, jnp.where(where == 1, total_high, total - total_high))

    for copy in copies[4:]:
        copy.wait()
    counts = [[] for _ in range(s.units)]
    for a in range(s.tile_rows):
        tile_row = row * s.tile_rows + a
        first = tile_row * s.unit_hosts
        member = members(hosts_ref[pl.ds(tile_row, 1), :], first, s.unit_hosts)
        sums = mm(member.astype(bf16), links_ref[a * s.tile : (a + 1) * s.tile, :])
        for b in range(s.units):
            unit = column * s.units + b
            target = hosts_ref[pl.ds(unit, 1), :]
            valid = ~members(target, first, s.unit_hosts) & (dangling_ref[pl.ds(unit, 1), :] == 0)
            stored = (tiles_ref[a, b] > 0).astype(f32)
            part = sums[:, b * s.tile : (b + 1) * s.tile]
            counts[b].append(jnp.where(valid, part, 0.0) * stored)
    for k in range(s.cols):
        chunk = column ^ k
        at = pl.multiple_of(chunk * s.piece, s.piece)
        for b in range(s.units):
            lanes = slice(b * s.tile, (b + 1) * s.tile)
            stored = (tiles_ref[chunk // s.pair, b] > 0).astype(f32).astype(bf16)
            chunk_refs[k][:, lanes] = links_ref[pl.ds(at, s.piece), lanes] * stored
    values = jnp.concatenate(
        [ranks.astype(bf16)]
        + [jnp.concatenate(c, axis=0).astype(bf16) for c in counts]
        + [extra.astype(bf16)],
        axis=0,
    )
    for n in range(s.rows):
        sent_ref[n] = values


def ranks_kernel(s, buffer_ref, local_ref):
    for n in range(s.rows):
        local_ref[n * s.piece : (n + 1) * s.piece, :] = buffer_ref[s.place_of(n), : s.piece, :]


def graph_kernel(s, buffer_ref, hosts_ref, local_ref, shared_ref):
    column = lax.axis_index("col")
    ones = jnp.ones((8, LANES), bf16)
    low = iota((1, LANES), 1) < s.piece
    extras = [buffer_ref[s.place_of(n), s.at_extra :, :].astype(f32) for n in range(s.rows)]
    total = functools.reduce(jnp.add, [e[1:2] + e[2:3] for e in extras])
    for m in range(s.units):
        unit = column * s.units + m
        member = members(hosts_ref[pl.ds(unit, 1), :], unit * s.unit_hosts, s.unit_hosts)
        start = s.at_counts + m * s.row_hosts
        counts = jnp.concatenate(
            [buffer_ref[s.place_of(n), start : start + s.row_hosts, :] for n in range(s.rows)], axis=0
        )
        ranks = local_ref[m * s.tile : (m + 1) * s.tile, :]
        inward = jnp.where(low, extras[s.pair * m][:1], extras[s.pair * m + 1][:1])
        degree = inward + mm(jnp.ones((8, s.hosts), bf16), counts)[:1]
        has_out = degree > 0
        inverse = jnp.where(has_out, 1.0 / jnp.where(has_out, degree, 1.0), 0.0)
        means = mm_nt(ones[:, : s.topics], ranks)[:1] * (1.0 / s.topics) * inverse
        weights = mm_nt((member.astype(f32) * means).astype(bf16), counts)
        out = jnp.sum(weights, axis=1, keepdims=True)
        linked = out > 0
        norm = jnp.where(linked, weights / jnp.where(linked, out, 1.0), 1.0 / s.hosts)
        shared_ref[m * s.unit_hosts : (m + 1) * s.unit_hosts, :] = norm
        shared_ref[s.column_hosts + m : s.column_hosts + m + 1, :LANES] = inverse
    shared_ref[s.column_hosts + s.units : s.column_hosts + s.units + 1, : s.topics] = total


def mask_kernel(s, hosts_ref, dangling_ref, out_ref):
    piece = lax.axis_index("row") * s.cols + lax.axis_index("col")
    unit, half = piece // s.pair, piece % s.pair
    hosts = hosts_ref[pl.ds(unit, 1), :]
    keep = dangling_ref[pl.ds(unit, 1), :] == 0
    mine = rows_of(hosts, half, s.piece)[:, : s.piece]
    first = piece * HOSTS_PIECE
    same = mm_tn(members(mine, first, 8).astype(bf16), members(hosts, first, 8).astype(bf16))
    out_ref[...] = same * jnp.where(keep, 1.0, -1.0)


def edges_kernel(s, own_ref, mask_ref, *refs):
    chunk_refs, out_ref = refs[: s.cols], refs[s.cols]
    column = lax.axis_index("col")
    for k in range(s.cols):
        at = pl.multiple_of((column ^ k) * s.width, s.width)
        out_ref[:, pl.ds(at, s.width)] = chunk_refs[k][...]
    unit = (lax.axis_index("row") * s.cols + column) // s.pair
    mask = mask_ref[...]
    packed = own_ref[s.piece :, :].astype(f32)
    rolled = pltpu.roll(packed, s.piece, 1)
    low = iota((s.packed, LANES), 1) < s.piece
    local = jnp.concatenate([jnp.where(low, packed, rolled), jnp.where(low, rolled, packed)], axis=0)
    at = pl.multiple_of(unit * s.tile, s.tile)
    across = out_ref[:, pl.ds(at, s.tile)].astype(f32)
    fixed = jnp.where(mask == 0, across, jnp.where(mask > 0, local, 0.0))
    out_ref[:, pl.ds(at, s.tile)] = fixed.astype(bf16)


def three(x):
    high = x.astype(bf16).astype(f32)
    rest = x - high
    middle = rest.astype(bf16).astype(f32)
    where = iota((8, x.shape[1]), 0)
    parts = jnp.where(where == 0, high, jnp.where(where == 1, middle, rest - middle))
    return jnp.where(where < 3, parts, 0.0).astype(bf16)


def host_kernel(s, own_ref, hosts_ref, edges_ref, *refs):
    shared, (weighted_ref, base_ref, full_ref, inverse_ref) = refs[: s.cols], refs[s.cols :]
    column = lax.axis_index("col")
    total = jnp.zeros((1, s.topics), f32)
    for k in range(s.cols):
        at = pl.multiple_of((column ^ k) * s.column_hosts, s.column_hosts)
        full_ref[pl.ds(at, s.column_hosts), :] = shared[k][: s.column_hosts, :]
        end = s.column_hosts + s.units
        inverse_ref[pl.ds((column ^ k) * s.units, s.units), :] = shared[k][s.column_hosts : end, :LANES]
        total = total + shared[k][end : end + 1, : s.topics]
    base_ref[...] = (1 - damping) * s.pages * own_ref[: s.piece, :].astype(f32) / total
    norm = full_ref[...]
    norm_high, norm_low = split(norm)
    rank = damping * jnp.sum(norm, axis=0, keepdims=True) + (1 - damping)
    for _ in range(HOST_ITERS - 1):
        parts = three(rank)
        fresh = mm(parts, norm_high) + mm(parts, norm_low)
        rank = damping * jnp.sum(fresh, axis=0, keepdims=True) + (1 - damping)
    block = LANES // s.unit_hosts
    all_units = s.units * s.cols
    for g in range(s.hosts // LANES):
        count = min(block, all_units - g * block)
        hosts = hosts_ref[g * block : g * block + count, :] - g * LANES
        ranks = jnp.broadcast_to(rank[:, g * LANES : (g + 1) * LANES], (count, LANES))
        page = damping * jnp.take_along_axis(ranks, hosts, axis=1)
        inverse = inverse_ref[g * block : g * block + count, :]
        scale = page * inverse
        dead = jnp.where(inverse > 0, 0.0, page * (1.0 / s.pages))
        for u in range(count):
            at = (g * block + u) * s.tile
            lanes = slice(at, at + s.tile)
            links = edges_ref[:, lanes].astype(f32)
            weighted_ref[:, lanes] = (links * scale[u : u + 1] + dead[u : u + 1]).astype(bf16)


def flow_kernel(s, distances, weighted_ref, base_ref, *refs):
    locals_, out_ref = refs[:-1], refs[-1]
    column = lax.axis_index("col")
    flow = base_ref[...]
    for k, local_ref in zip(distances, locals_, strict=True):
        at = pl.multiple_of((column ^ k) * s.width, s.width)
        flow = flow + mm(weighted_ref[:, pl.ds(at, s.width)], local_ref[...])
    out_ref[...] = flow


def in_hbm(x):
    return pltpu.with_memory_space_constraint(x, pltpu.HBM)


def swap(x, count, bits):
    return lax.ppermute(x, "col", [(i, i ^ bits) for i in range(count)])


def gathered(x, count):
    found = {0: x}
    bit = count // 2
    while bit:
        for k, v in list(found.items()):
            found[k ^ bit] = swap(v, count, bit)
        bit //= 2
    return [found[k] for k in range(count)]


def spread(values, count):
    found = [values[0]]
    for k in range(1, count):
        found.append(swap(values[k], count, k))
    return found


def call(kernel, out_shape, in_specs, scratch=(), cost=10**6):
    single = not isinstance(out_shape, tuple)
    return pl.pallas_call(
        kernel,
        out_shape=out_shape,
        in_specs=in_specs,
        out_specs=VMEM if single else (VMEM,) * len(out_shape),
        scratch_shapes=scratch,
        compiler_params=pltpu.CompilerParams(vmem_limit_bytes=GRANT),
        cost_estimate=pl.CostEstimate(flops=cost, bytes_accessed=cost, transcendentals=0),
    )


def on_device(links, tiles, local_links, host_ids, dangling, teleport):
    rows, cols = lax.axis_size("row"), lax.axis_size("col")
    pages = host_ids.shape[0]
    s = Sizes(rows, cols, links.shape, tiles.shape, local_links.shape, teleport.shape, pages)
    hosts = host_ids.reshape(pages // LANES, LANES)
    ignored = dangling.reshape(pages // LANES, LANES)
    shape = jax.ShapeDtypeStruct
    sent, own, *chunks = call(
        functools.partial(first_kernel, s),
        (
            shape((rows, s.payload, LANES), bf16),
            shape((s.piece + s.packed, LANES), bf16),
            *(shape((s.piece, s.width), bf16) for _ in range(cols)),
        ),
        [HBM] * 6,
        [pltpu.SMEM(tiles.shape, tiles.dtype)]
        + [pltpu.VMEM(a.shape, a.dtype) for a in (links, hosts, ignored, local_links, teleport)]
        + [pltpu.SemaphoreType.DMA((6,))],
    )(*(in_hbm(x) for x in (tiles, links, hosts, ignored, local_links, teleport)))
    moves = [(r * cols + c, c * rows + r) for r in range(rows) for c in range(cols)]
    own = lax.ppermute(own, ("row", "col"), moves)
    chunks = spread(chunks, cols)
    group = [s.row_at(p) for p in range(rows)]
    held = lax.all_to_all(sent, "row", 0, 0, tiled=True, axis_index_groups=[group])
    local = call(functools.partial(ranks_kernel, s), shape((s.width, s.topics), bf16), [VMEM])(held)
    locals_ = gathered(local, cols)
    shared = call(
        functools.partial(graph_kernel, s),
        shape((s.column_hosts + s.extra, s.hosts), f32),
        [VMEM] * 3,
    )(held, hosts, local)
    shared = spread([shared] * cols, cols)
    mask = call(
        functools.partial(mask_kernel, s), shape((s.piece, s.tile), f32), [VMEM] * 2
    )(hosts, ignored)
    edges = call(
        functools.partial(edges_kernel, s),
        shape((s.piece, pages), bf16),
        [VMEM] * (2 + cols),
    )(own, mask, *chunks)
    weighted, base = call(
        functools.partial(host_kernel, s),
        (shape((s.piece, pages), bf16), shape((s.piece, s.topics), f32)),
        [VMEM] * (3 + cols),
        [pltpu.VMEM((s.hosts, s.hosts), f32), pltpu.VMEM((s.units * cols, LANES), f32)],
    )(own, hosts, edges, *shared)
    late = [k for k in range(cols) if k % 2 and k > 1]
    soon = [k for k in range(cols) if k not in late]
    flow = base
    for distances in (soon, late):
        flow = call(
            functools.partial(flow_kernel, s, distances),
            shape((s.piece, s.topics), f32),
            [VMEM] * (2 + len(distances)),
        )(weighted, flow, *(locals_[k] for k in distances))
    return flow


def solution(mesh):
    return jax.shard_map(
        on_device,
        mesh=mesh,
        in_specs=(
            P("row", "col"),
            P("row", "col"),
            P(("col", "row"), None),
            P(),
            P(),
            P(("col", "row"), None),
        ),
        out_specs=P(("row", "col"), None),
        check_vma=False,
    )
```

```python
import functools

import jax
import jax.numpy as jnp
from jax import lax
from jax.experimental import pallas as pl
from jax.experimental.pallas import tpu as pltpu
from jax.sharding import PartitionSpec as P


HOSTS_PIECE = 4
LOCAL_ITERS = 2
HOST_ITERS = 3
LANES = 128
GRANT = 24 * 2**20

damping = 0.85
f32 = jnp.float32
bf16 = jnp.bfloat16

VMEM = pl.BlockSpec(memory_space=pltpu.VMEM)
SMEM = pl.BlockSpec(memory_space=pltpu.SMEM)
HBM = pl.BlockSpec(memory_space=pltpu.HBM)


def iota(shape, axis):
    return lax.broadcasted_iota(jnp.int32, shape, axis)


def mm(a, b):
    return jnp.dot(a, b, preferred_element_type=f32)


def mm_nt(a, b):
    return lax.dot_general(a, b, (((1,), (1,)), ((), ())), preferred_element_type=f32)


def mm_tn(a, b):
    return lax.dot_general(a, b, (((0,), (0,)), ((), ())), preferred_element_type=f32)


def split(x):
    high = x.astype(bf16)
    return high, (x - high.astype(f32)).astype(bf16)


def members(hosts_row, first, count):
    return hosts_row == first + iota((count, hosts_row.shape[1]), 0)


class Sizes:
    def __init__(self, rows, cols, links, tiles, local_links, teleport, pages):
        self.rows, self.cols, self.pages = rows, cols, pages
        self.height, self.width = links
        self.piece = local_links[0]
        self.topics = teleport[1]
        self.tile = self.height // tiles[0]
        self.tile_rows, self.units = tiles
        self.pair = self.tile // self.piece
        self.unit_hosts = self.pair * HOSTS_PIECE
        self.hosts = HOSTS_PIECE * rows * cols
        self.column_hosts = HOSTS_PIECE * rows
        self.row_hosts = HOSTS_PIECE * cols
        self.packed = self.piece * self.piece // LANES
        self.at_counts = self.piece
        self.at_extra = self.at_counts + self.units * self.row_hosts
        self.payload = self.at_extra + 8
        self.extra = (2 * self.units + 2 + 15) // 16 * 16

    def row_at(self, place):
        return (place + self.rows // 2) % self.rows

    def place_of(self, row):
        return (row - self.rows // 2) % self.rows


def rows_of(row, half, piece):
    rolled = pltpu.roll(row, piece, 1)
    low = iota(row.shape, 1) < piece
    first = jnp.where(low, row, rolled)
    second = jnp.where(low, rolled, row)
    return jnp.where(half == 0, first, second)


def first_kernel(s, tiles_hbm, links_hbm, hosts_hbm, dangling_hbm, local_hbm, teleport_hbm, *refs):
    sent_ref, own_ref, chunk_refs = refs[0], refs[1], refs[2 : 2 + s.cols]
    tiles_ref, links_ref, hosts_ref, dangling_ref, local_ref, teleport_ref, sem = refs[2 + s.cols :]
    copies = [
        pltpu.make_async_copy(source, target, sem.at[i])
        for i, (source, target) in enumerate(
            (
                (hosts_hbm, hosts_ref),
                (dangling_hbm, dangling_ref),
                (local_hbm, local_ref),
                (teleport_hbm, teleport_ref),
                (links_hbm, links_ref),
                (tiles_hbm, tiles_ref),
            )
        )
    ]
    for copy in copies:
        copy.start()
    row, column = lax.axis_index("row"), lax.axis_index("col")
    for copy in copies[:4]:
        copy.wait()
    piece = column * s.rows + row
    unit, half = piece // s.pair, piece % s.pair
    hosts = rows_of(hosts_ref[pl.ds(unit, 1), :], half, s.piece)[:, : s.piece]
    keep = rows_of(dangling_ref[pl.ds(unit, 1), :], half, s.piece)[:, : s.piece] == 0
    member = members(hosts, piece * HOSTS_PIECE, 8).astype(bf16)
    same = mm_tn(member, member)
    sameb = same.astype(bf16)
    local = local_ref[...].astype(f32)
    inside = local * same * keep.astype(f32)
    inward = jnp.sum(inside, axis=0, keepdims=True)
    size = jnp.sum(same, axis=0, keepdims=True)
    live = inward > 0
    step = inside * jnp.where(live, 1.0 / jnp.where(live, inward, 1.0), 0.0)
    step = step + same * jnp.where(live, 0.0, 1.0 / size)
    high, low = split(step)
    teleport = teleport_ref[...]
    tele_high, tele_low = split(teleport)
    sizes = jnp.sum(same, axis=1, keepdims=True)
    restart = sizes * teleport / (mm(sameb, tele_high) + mm(sameb, tele_low))
    ranks = damping * jnp.sum(step, axis=1, keepdims=True) + (1 - damping) * restart
    for _ in range(LOCAL_ITERS - 1):
        ranks_high, ranks_low = split(ranks)
        flow = mm(high, ranks_high) + mm(high, ranks_low) + mm(low, ranks_high)
        ranks = damping * flow + (1 - damping) * restart
    half_piece = s.piece // 2
    packed = jnp.concatenate([local[:half_piece], local[half_piece:]], axis=1).astype(bf16)
    own_ref[: s.piece, :] = tele_high
    own_ref[s.piece :, :] = packed
    total = jnp.sum(teleport, axis=0, keepdims=True)
    total_high = total.astype(bf16).astype(f32)
    where = iota((8, LANES), 0)
    inward = jnp.concatenate([inward, inward], axis=1)
    extra = jnp.where(where == 0, inward, jnp.where(where == 1, total_high, total - total_high))

    for copy in copies[4:]:
        copy.wait()
    counts = [[] for _ in range(s.units)]
    for a in range(s.tile_rows):
        tile_row = row * s.tile_rows + a
        first = tile_row * s.unit_hosts
        member = members(hosts_ref[pl.ds(tile_row, 1), :], first, s.unit_hosts)
        sums = mm(member.astype(bf16), links_ref[a * s.tile : (a + 1) * s.tile, :])
        for b in range(s.units):
            unit = column * s.units + b
            target = hosts_ref[pl.ds(unit, 1), :]
            valid = ~members(target, first, s.unit_hosts) & (dangling_ref[pl.ds(unit, 1), :] == 0)
            stored = (tiles_ref[a, b] > 0).astype(f32)
            part = sums[:, b * s.tile : (b + 1) * s.tile]
            counts[b].append(jnp.where(valid, part, 0.0) * stored)
    for k in range(s.cols):
        chunk = column ^ k
        at = pl.multiple_of(chunk * s.piece, s.piece)
        for b in range(s.units):
            lanes = slice(b * s.tile, (b + 1) * s.tile)
            stored = (tiles_ref[chunk // s.pair, b] > 0).astype(f32).astype(bf16)
            chunk_refs[k][:, lanes] = links_ref[pl.ds(at, s.piece), lanes] * stored
    values = jnp.concatenate(
        [ranks.astype(bf16)]
        + [jnp.concatenate(c, axis=0).astype(bf16) for c in counts]
        + [extra.astype(bf16)],
        axis=0,
    )
    for n in range(s.rows):
        sent_ref[n] = values


def ranks_kernel(s, buffer_ref, local_ref):
    for n in range(s.rows):
        local_ref[n * s.piece : (n + 1) * s.piece, :] = buffer_ref[s.place_of(n), : s.piece, :]


def graph_kernel(s, buffer_ref, hosts_ref, local_ref, shared_ref):
    column = lax.axis_index("col")
    low = iota((1, LANES), 1) < s.piece
    extras = [buffer_ref[s.place_of(n), s.at_extra :, :].astype(f32) for n in range(s.rows)]
    total = functools.reduce(jnp.add, [e[1:2] + e[2:3] for e in extras])
    square = (s.tile, s.tile)
    diagonal = iota(square, 0) == iota(square, 1)
    lines = []
    for m in range(s.units):
        unit = column * s.units + m
        member = members(hosts_ref[pl.ds(unit, 1), :], unit * s.unit_hosts, s.unit_hosts)
        start = s.at_counts + m * s.row_hosts
        counts = jnp.concatenate(
            [buffer_ref[s.place_of(n), start : start + s.row_hosts, :] for n in range(s.rows)], axis=0
        )
        extra = jnp.where(low, extras[s.pair * m], extras[s.pair * m + 1])
        outward = jnp.sum(counts.astype(f32), axis=0, keepdims=True)
        degree = extra[:1] + outward
        has_out = degree > 0
        inverse = jnp.where(has_out, 1.0 / jnp.where(has_out, degree, 1.0), 0.0)
        ranks = local_ref[m * s.tile : (m + 1) * s.tile, :].astype(f32)
        sums = jnp.sum(ranks, axis=1, keepdims=True)
        sums = jnp.sum(jnp.where(diagonal, sums, 0.0), axis=0, keepdims=True)
        means = sums * (1.0 / s.topics) * inverse
        spread = (member.astype(f32) * means).astype(bf16)
        weights = mm_nt(spread, counts)
        out = jnp.sum(spread.astype(f32) * outward, axis=1, keepdims=True)
        linked = out > 0
        norm = jnp.where(linked, weights * (1.0 / jnp.where(linked, out, 1.0)), 1.0 / s.hosts)
        shared_ref[m * s.unit_hosts : (m + 1) * s.unit_hosts, :] = norm.astype(bf16)
        high = inverse.astype(bf16).astype(f32)
        lines += [high, inverse - high]
    high = total.astype(bf16).astype(f32)
    lines += [high, total - high]
    lines += [jnp.zeros((1, LANES), f32)] * (s.extra - len(lines))
    shared_ref[s.column_hosts :, :LANES] = jnp.concatenate(lines, axis=0).astype(bf16)


def mask_kernel(s, hosts_ref, dangling_ref, out_ref):
    piece = lax.axis_index("row") * s.cols + lax.axis_index("col")
    unit, half = piece // s.pair, piece % s.pair
    hosts = hosts_ref[pl.ds(unit, 1), :]
    keep = dangling_ref[pl.ds(unit, 1), :] == 0
    mine = rows_of(hosts, half, s.piece)[:, : s.piece]
    first = piece * HOSTS_PIECE
    same = mm_tn(members(mine, first, 8).astype(bf16), members(hosts, first, 8).astype(bf16))
    out_ref[...] = same * jnp.where(keep, 1.0, -1.0)


def edges_kernel(s, own_ref, mask_ref, *refs):
    chunk_refs, out_ref = refs[: s.cols], refs[s.cols]
    column = lax.axis_index("col")
    for k in range(s.cols):
        at = pl.multiple_of((column ^ k) * s.width, s.width)
        out_ref[:, pl.ds(at, s.width)] = chunk_refs[k][...]
    unit = (lax.axis_index("row") * s.cols + column) // s.pair
    mask = mask_ref[...]
    packed = own_ref[s.piece :, :].astype(f32)
    rolled = pltpu.roll(packed, s.piece, 1)
    low = iota((s.packed, LANES), 1) < s.piece
    local = jnp.concatenate([jnp.where(low, packed, rolled), jnp.where(low, rolled, packed)], axis=0)
    at = pl.multiple_of(unit * s.tile, s.tile)
    across = out_ref[:, pl.ds(at, s.tile)].astype(f32)
    fixed = jnp.where(mask == 0, across, jnp.where(mask > 0, local, 0.0))
    out_ref[:, pl.ds(at, s.tile)] = fixed.astype(bf16)


def three(x):
    high = x.astype(bf16).astype(f32)
    rest = x - high
    middle = rest.astype(bf16).astype(f32)
    where = iota((8, x.shape[1]), 0)
    parts = jnp.where(where == 0, high, jnp.where(where == 1, middle, rest - middle))
    return jnp.where(where < 3, parts, 0.0).astype(bf16)


def host_kernel(s, own_ref, hosts_ref, edges_ref, *refs):
    shared, (weighted_ref, base_ref, full_ref, inverse_ref) = refs[: s.cols], refs[s.cols :]
    column = lax.axis_index("col")
    total = jnp.zeros((1, s.topics), f32)
    for k in range(s.cols):
        at = pl.multiple_of((column ^ k) * s.column_hosts, s.column_hosts)
        full_ref[pl.ds(at, s.column_hosts), :] = shared[k][: s.column_hosts, :]
        lines = shared[k][s.column_hosts :, :LANES].astype(f32)
        for m in range(s.units):
            line = lines[2 * m : 2 * m + 1] + lines[2 * m + 1 : 2 * m + 2]
            inverse_ref[pl.ds((column ^ k) * s.units + m, 1), :] = line
        total = total + lines[2 * s.units : 2 * s.units + 1] + lines[2 * s.units + 1 : 2 * s.units + 2]
    base_ref[...] = (1 - damping) * s.pages * own_ref[: s.piece, :].astype(f32) / total
    norm = full_ref[...]
    parts = jnp.where(iota((8, s.hosts), 0) == 0, 1.0, 0.0).astype(bf16)
    for step in range(HOST_ITERS):
        if step:
            parts = three(rank)
        rank = damping * jnp.sum(mm(parts, norm), axis=0, keepdims=True) + (1 - damping)
    block = LANES // s.unit_hosts
    all_units = s.units * s.cols
    for g in range(s.hosts // LANES):
        count = min(block, all_units - g * block)
        hosts = hosts_ref[g * block : g * block + count, :] - g * LANES
        ranks = jnp.broadcast_to(rank[:, g * LANES : (g + 1) * LANES], (count, LANES))
        page = damping * jnp.take_along_axis(ranks, hosts, axis=1)
        inverse = inverse_ref[g * block : g * block + count, :]
        scale = page * inverse
        dead = jnp.where(inverse > 0, 0.0, page * (1.0 / s.pages))
        for u in range(count):
            at = (g * block + u) * s.tile
            lanes = slice(at, at + s.tile)
            links = edges_ref[:, lanes].astype(f32)
            weighted_ref[:, lanes] = (links * scale[u : u + 1] + dead[u : u + 1]).astype(bf16)


def flow_kernel(s, distances, weighted_ref, base_ref, *refs):
    locals_, out_ref = refs[:-1], refs[-1]
    column = lax.axis_index("col")
    flow = base_ref[...]
    for k, local_ref in zip(distances, locals_, strict=True):
        at = pl.multiple_of((column ^ k) * s.width, s.width)
        flow = flow + mm(weighted_ref[:, pl.ds(at, s.width)], local_ref[...])
    out_ref[...] = flow


def in_hbm(x):
    return pltpu.with_memory_space_constraint(x, pltpu.HBM)


def swap(x, count, bits):
    return lax.ppermute(x, "col", [(i, i ^ bits) for i in range(count)])


def gathered(x, count):
    found = {0: x}
    bit = count // 2
    while bit:
        for k, v in list(found.items()):
            found[k ^ bit] = swap(v, count, bit)
        bit //= 2
    return [found[k] for k in range(count)]


def spread(values, count):
    found = [values[0]]
    for k in range(1, count):
        found.append(swap(values[k], count, k))
    return found


def call(kernel, out_shape, in_specs, scratch=(), cost=10**6):
    single = not isinstance(out_shape, tuple)
    return pl.pallas_call(
        kernel,
        out_shape=out_shape,
        in_specs=in_specs,
        out_specs=VMEM if single else (VMEM,) * len(out_shape),
        scratch_shapes=scratch,
        compiler_params=pltpu.CompilerParams(vmem_limit_bytes=GRANT),
        cost_estimate=pl.CostEstimate(flops=cost, bytes_accessed=cost, transcendentals=0),
    )


def on_device(links, tiles, local_links, host_ids, dangling, teleport):
    rows, cols = lax.axis_size("row"), lax.axis_size("col")
    pages = host_ids.shape[0]
    s = Sizes(rows, cols, links.shape, tiles.shape, local_links.shape, teleport.shape, pages)
    hosts = host_ids.reshape(pages // LANES, LANES)
    ignored = dangling.reshape(pages // LANES, LANES)
    shape = jax.ShapeDtypeStruct
    sent, own, *chunks = call(
        functools.partial(first_kernel, s),
        (
            shape((rows, s.payload, LANES), bf16),
            shape((s.piece + s.packed, LANES), bf16),
            *(shape((s.piece, s.width), bf16) for _ in range(cols)),
        ),
        [HBM] * 6,
        [pltpu.SMEM(tiles.shape, tiles.dtype)]
        + [pltpu.VMEM(a.shape, a.dtype) for a in (links, hosts, ignored, local_links, teleport)]
        + [pltpu.SemaphoreType.DMA((6,))],
    )(*(in_hbm(x) for x in (tiles, links, hosts, ignored, local_links, teleport)))
    moves = [(r * cols + c, c * rows + r) for r in range(rows) for c in range(cols)]
    own = lax.ppermute(own, ("row", "col"), moves)
    chunks = spread(chunks, cols)
    group = [s.row_at(p) for p in range(rows)]
    held = lax.all_to_all(sent, "row", 0, 0, tiled=True, axis_index_groups=[group])
    local = call(functools.partial(ranks_kernel, s), shape((s.width, s.topics), bf16), [VMEM])(held)
    locals_ = gathered(local, cols)
    shared = call(
        functools.partial(graph_kernel, s),
        shape((s.column_hosts + s.extra, s.hosts), bf16),
        [VMEM] * 3,
    )(held, hosts, local)
    shared = spread([shared] * cols, cols)
    mask = call(
        functools.partial(mask_kernel, s), shape((s.piece, s.tile), f32), [VMEM] * 2
    )(hosts, ignored)
    edges = call(
        functools.partial(edges_kernel, s),
        shape((s.piece, pages), bf16),
        [VMEM] * (2 + cols),
    )(own, mask, *chunks)
    weighted, base = call(
        functools.partial(host_kernel, s),
        (shape((s.piece, pages), bf16), shape((s.piece, s.topics), f32)),
        [VMEM] * (3 + cols),
        [pltpu.VMEM((s.hosts, s.hosts), bf16), pltpu.VMEM((s.units * cols, LANES), f32)],
    )(own, hosts, edges, *shared)
    late = [k for k in range(cols) if k % 2 and k > 1]
    soon = [k for k in range(cols) if k not in late]
    flow = base
    for distances in (soon, late):
        flow = call(
            functools.partial(flow_kernel, s, distances),
            shape((s.piece, s.topics), f32),
            [VMEM] * (2 + len(distances)),
        )(weighted, flow, *(locals_[k] for k in distances))
    return flow


def solution(mesh):
    return jax.shard_map(
        on_device,
        mesh=mesh,
        in_specs=(
            P("row", "col"),
            P("row", "col"),
            P(("col", "row"), None),
            P(),
            P(),
            P(("col", "row"), None),
        ),
        out_specs=P(("row", "col"), None),
        check_vma=False,
    )
```

```python
import functools

import jax
import jax.numpy as jnp
from jax import lax
from jax.experimental import pallas as pl
from jax.experimental.pallas import tpu as pltpu
from jax.sharding import PartitionSpec as P


HOSTS_PIECE = 4
LOCAL_ITERS = 2
HOST_ITERS = 3
LANES = 128
ROW_ORDERS = {8: (4, 0, 7, 5, 3, 1, 6, 2)}
GRANT = 24 * 2**20

damping = 0.85
f32 = jnp.float32
bf16 = jnp.bfloat16

VMEM = pl.BlockSpec(memory_space=pltpu.VMEM)
SMEM = pl.BlockSpec(memory_space=pltpu.SMEM)
HBM = pl.BlockSpec(memory_space=pltpu.HBM)


def iota(shape, axis):
    return lax.broadcasted_iota(jnp.int32, shape, axis)


def mm(a, b):
    return jnp.dot(a, b, preferred_element_type=f32)


def mm_nt(a, b):
    return lax.dot_general(a, b, (((1,), (1,)), ((), ())), preferred_element_type=f32)


def mm_tn(a, b):
    return lax.dot_general(a, b, (((0,), (0,)), ((), ())), preferred_element_type=f32)


def split(x):
    high = x.astype(bf16)
    return high, (x - high.astype(f32)).astype(bf16)


def members(hosts_row, first, count):
    return hosts_row == first + iota((count, hosts_row.shape[1]), 0)


class Sizes:
    def __init__(self, rows, cols, links, tiles, local_links, teleport, pages):
        self.rows, self.cols, self.pages = rows, cols, pages
        self.height, self.width = links
        self.piece = local_links[0]
        self.topics = teleport[1]
        self.tile = self.height // tiles[0]
        self.tile_rows, self.units = tiles
        self.pair = self.tile // self.piece
        self.unit_hosts = self.pair * HOSTS_PIECE
        self.hosts = HOSTS_PIECE * rows * cols
        self.column_hosts = HOSTS_PIECE * rows
        self.row_hosts = HOSTS_PIECE * cols
        self.packed = self.piece * self.piece // LANES
        self.at_counts = self.piece
        self.at_extra = self.at_counts + self.units * self.row_hosts
        self.payload = self.at_extra + 8
        self.extra = (2 * self.units + 2 + 15) // 16 * 16

    def row_at(self, place):
        listed = ROW_ORDERS.get(self.rows)
        return listed[place] if listed else (place + self.rows // 2) % self.rows

    def place_of(self, row):
        return [self.row_at(place) for place in range(self.rows)].index(row)


def rows_of(row, half, piece):
    rolled = pltpu.roll(row, piece, 1)
    low = iota(row.shape, 1) < piece
    first = jnp.where(low, row, rolled)
    second = jnp.where(low, rolled, row)
    return jnp.where(half == 0, first, second)


def first_kernel(s, tiles_hbm, links_hbm, hosts_hbm, dangling_hbm, local_hbm, teleport_hbm, *refs):
    sent_ref, own_ref, chunk_refs = refs[0], refs[1], refs[2 : 2 + s.cols]
    tiles_ref, links_ref, hosts_ref, dangling_ref, local_ref, teleport_ref, sem = refs[2 + s.cols :]
    copies = [
        pltpu.make_async_copy(source, target, sem.at[i])
        for i, (source, target) in enumerate(
            (
                (hosts_hbm, hosts_ref),
                (dangling_hbm, dangling_ref),
                (local_hbm, local_ref),
                (teleport_hbm, teleport_ref),
                (links_hbm, links_ref),
                (tiles_hbm, tiles_ref),
            )
        )
    ]
    for copy in copies:
        copy.start()
    row, column = lax.axis_index("row"), lax.axis_index("col")
    for copy in copies[:4]:
        copy.wait()
    piece = column * s.rows + row
    unit, half = piece // s.pair, piece % s.pair
    hosts = rows_of(hosts_ref[pl.ds(unit, 1), :], half, s.piece)[:, : s.piece]
    keep = rows_of(dangling_ref[pl.ds(unit, 1), :], half, s.piece)[:, : s.piece] == 0
    member = members(hosts, piece * HOSTS_PIECE, 8).astype(bf16)
    same = mm_tn(member, member)
    sameb = same.astype(bf16)
    local = local_ref[...].astype(f32)
    inside = local * same * keep.astype(f32)
    inward = jnp.sum(inside, axis=0, keepdims=True)
    size = jnp.sum(same, axis=0, keepdims=True)
    live = inward > 0
    step = inside * jnp.where(live, 1.0 / jnp.where(live, inward, 1.0), 0.0)
    step = step + same * jnp.where(live, 0.0, 1.0 / size)
    high, low = split(step)
    teleport = teleport_ref[...]
    tele_high, tele_low = split(teleport)
    sizes = jnp.sum(same, axis=1, keepdims=True)
    restart = sizes * teleport / (mm(sameb, tele_high) + mm(sameb, tele_low))
    ranks = damping * jnp.sum(step, axis=1, keepdims=True) + (1 - damping) * restart
    for _ in range(LOCAL_ITERS - 1):
        ranks_high, ranks_low = split(ranks)
        flow = mm(high, ranks_high) + mm(high, ranks_low) + mm(low, ranks_high)
        ranks = damping * flow + (1 - damping) * restart
    half_piece = s.piece // 2
    packed = jnp.concatenate([local[:half_piece], local[half_piece:]], axis=1).astype(bf16)
    own_ref[: s.piece, :] = tele_high
    own_ref[s.piece :, :] = packed
    total = jnp.sum(teleport, axis=0, keepdims=True)
    total_high = total.astype(bf16).astype(f32)
    where = iota((8, LANES), 0)
    inward = jnp.concatenate([inward, inward], axis=1)
    extra = jnp.where(where == 0, inward, jnp.where(where == 1, total_high, total - total_high))

    for copy in copies[4:]:
        copy.wait()
    counts = [[] for _ in range(s.units)]
    for a in range(s.tile_rows):
        tile_row = row * s.tile_rows + a
        first = tile_row * s.unit_hosts
        member = members(hosts_ref[pl.ds(tile_row, 1), :], first, s.unit_hosts)
        sums = mm(member.astype(bf16), links_ref[a * s.tile : (a + 1) * s.tile, :])
        for b in range(s.units):
            unit = column * s.units + b
            target = hosts_ref[pl.ds(unit, 1), :]
            valid = ~members(target, first, s.unit_hosts) & (dangling_ref[pl.ds(unit, 1), :] == 0)
            stored = (tiles_ref[a, b] > 0).astype(f32)
            part = sums[:, b * s.tile : (b + 1) * s.tile]
            counts[b].append(jnp.where(valid, part, 0.0) * stored)
    for k in range(s.cols):
        chunk = column ^ k
        at = pl.multiple_of(chunk * s.piece, s.piece)
        for b in range(s.units):
            lanes = slice(b * s.tile, (b + 1) * s.tile)
            stored = (tiles_ref[chunk // s.pair, b] > 0).astype(f32).astype(bf16)
            chunk_refs[k][:, lanes] = links_ref[pl.ds(at, s.piece), lanes] * stored
    values = jnp.concatenate(
        [ranks.astype(bf16)]
        + [jnp.concatenate(c, axis=0).astype(bf16) for c in counts]
        + [extra.astype(bf16)],
        axis=0,
    )
    for n in range(s.rows):
        sent_ref[n] = values


def ranks_kernel(s, buffer_ref, local_ref):
    for n in range(s.rows):
        local_ref[n * s.piece : (n + 1) * s.piece, :] = buffer_ref[s.place_of(n), : s.piece, :]


def graph_kernel(s, buffer_ref, hosts_ref, local_ref, shared_ref):
    column = lax.axis_index("col")
    low = iota((1, LANES), 1) < s.piece
    extras = [buffer_ref[s.place_of(n), s.at_extra :, :].astype(f32) for n in range(s.rows)]
    total = functools.reduce(jnp.add, [e[1:2] + e[2:3] for e in extras])
    square = (s.tile, s.tile)
    diagonal = iota(square, 0) == iota(square, 1)
    lines = []
    for m in range(s.units):
        unit = column * s.units + m
        member = members(hosts_ref[pl.ds(unit, 1), :], unit * s.unit_hosts, s.unit_hosts)
        start = s.at_counts + m * s.row_hosts
        counts = jnp.concatenate(
            [buffer_ref[s.place_of(n), start : start + s.row_hosts, :] for n in range(s.rows)], axis=0
        )
        extra = jnp.where(low, extras[s.pair * m], extras[s.pair * m + 1])
        outward = jnp.sum(counts.astype(f32), axis=0, keepdims=True)
        degree = extra[:1] + outward
        has_out = degree > 0
        inverse = jnp.where(has_out, 1.0 / jnp.where(has_out, degree, 1.0), 0.0)
        ranks = local_ref[m * s.tile : (m + 1) * s.tile, :].astype(f32)
        sums = jnp.sum(ranks, axis=1, keepdims=True)
        sums = jnp.sum(jnp.where(diagonal, sums, 0.0), axis=0, keepdims=True)
        means = sums * (1.0 / s.topics) * inverse
        spread = (member.astype(f32) * means).astype(bf16)
        weights = mm_nt(spread, counts)
        out = jnp.sum(spread.astype(f32) * outward, axis=1, keepdims=True)
        linked = out > 0
        norm = jnp.where(linked, weights * (1.0 / jnp.where(linked, out, 1.0)), 1.0 / s.hosts)
        shared_ref[m * s.unit_hosts : (m + 1) * s.unit_hosts, :] = norm.astype(bf16)
        high = inverse.astype(bf16).astype(f32)
        lines += [high, inverse - high]
    high = total.astype(bf16).astype(f32)
    lines += [high, total - high]
    lines += [jnp.zeros((1, LANES), f32)] * (s.extra - len(lines))
    shared_ref[s.column_hosts :, :LANES] = jnp.concatenate(lines, axis=0).astype(bf16)


def mask_kernel(s, hosts_ref, dangling_ref, out_ref):
    piece = lax.axis_index("row") * s.cols + lax.axis_index("col")
    unit, half = piece // s.pair, piece % s.pair
    hosts = hosts_ref[pl.ds(unit, 1), :]
    keep = dangling_ref[pl.ds(unit, 1), :] == 0
    mine = rows_of(hosts, half, s.piece)[:, : s.piece]
    first = piece * HOSTS_PIECE
    same = mm_tn(members(mine, first, 8).astype(bf16), members(hosts, first, 8).astype(bf16))
    out_ref[...] = same * jnp.where(keep, 1.0, -1.0)


def edges_kernel(s, own_ref, mask_ref, *refs):
    chunk_refs, out_ref = refs[: s.cols], refs[s.cols]
    column = lax.axis_index("col")
    for k in range(s.cols):
        at = pl.multiple_of((column ^ k) * s.width, s.width)
        out_ref[:, pl.ds(at, s.width)] = chunk_refs[k][...]
    unit = (lax.axis_index("row") * s.cols + column) // s.pair
    mask = mask_ref[...]
    packed = own_ref[s.piece :, :].astype(f32)
    rolled = pltpu.roll(packed, s.piece, 1)
    low = iota((s.packed, LANES), 1) < s.piece
    local = jnp.concatenate([jnp.where(low, packed, rolled), jnp.where(low, rolled, packed)], axis=0)
    at = pl.multiple_of(unit * s.tile, s.tile)
    across = out_ref[:, pl.ds(at, s.tile)].astype(f32)
    fixed = jnp.where(mask == 0, across, jnp.where(mask > 0, local, 0.0))
    out_ref[:, pl.ds(at, s.tile)] = fixed.astype(bf16)


def three(x):
    high = x.astype(bf16).astype(f32)
    rest = x - high
    middle = rest.astype(bf16).astype(f32)
    where = iota((8, x.shape[1]), 0)
    parts = jnp.where(where == 0, high, jnp.where(where == 1, middle, rest - middle))
    return jnp.where(where < 3, parts, 0.0).astype(bf16)


def host_kernel(s, own_ref, hosts_ref, edges_ref, *refs):
    shared, (weighted_ref, base_ref, full_ref, inverse_ref) = refs[: s.cols], refs[s.cols :]
    column = lax.axis_index("col")
    total = jnp.zeros((1, s.topics), f32)
    for k in range(s.cols):
        at = pl.multiple_of((column ^ k) * s.column_hosts, s.column_hosts)
        full_ref[pl.ds(at, s.column_hosts), :] = shared[k][: s.column_hosts, :]
        lines = shared[k][s.column_hosts :, :LANES].astype(f32)
        for m in range(s.units):
            line = lines[2 * m : 2 * m + 1] + lines[2 * m + 1 : 2 * m + 2]
            inverse_ref[pl.ds((column ^ k) * s.units + m, 1), :] = line
        total = total + lines[2 * s.units : 2 * s.units + 1] + lines[2 * s.units + 1 : 2 * s.units + 2]
    base_ref[...] = (1 - damping) * s.pages * own_ref[: s.piece, :].astype(f32) / total
    norm = full_ref[...]
    parts = jnp.where(iota((8, s.hosts), 0) == 0, 1.0, 0.0).astype(bf16)
    for step in range(HOST_ITERS):
        if step:
            parts = three(rank)
        rank = damping * jnp.sum(mm(parts, norm), axis=0, keepdims=True) + (1 - damping)
    block = LANES // s.unit_hosts
    all_units = s.units * s.cols
    for g in range(s.hosts // LANES):
        count = min(block, all_units - g * block)
        hosts = hosts_ref[g * block : g * block + count, :] - g * LANES
        ranks = jnp.broadcast_to(rank[:, g * LANES : (g + 1) * LANES], (count, LANES))
        page = damping * jnp.take_along_axis(ranks, hosts, axis=1)
        inverse = inverse_ref[g * block : g * block + count, :]
        scale = page * inverse
        dead = jnp.where(inverse > 0, 0.0, page * (1.0 / s.pages))
        for u in range(count):
            at = (g * block + u) * s.tile
            lanes = slice(at, at + s.tile)
            links = edges_ref[:, lanes].astype(f32)
            weighted_ref[:, lanes] = (links * scale[u : u + 1] + dead[u : u + 1]).astype(bf16)


def flow_kernel(s, distances, weighted_ref, base_ref, *refs):
    locals_, out_ref = refs[:-1], refs[-1]
    column = lax.axis_index("col")
    flow = base_ref[...]
    for k, local_ref in zip(distances, locals_, strict=True):
        at = pl.multiple_of((column ^ k) * s.width, s.width)
        flow = flow + mm(weighted_ref[:, pl.ds(at, s.width)], local_ref[...])
    out_ref[...] = flow


def in_hbm(x):
    return pltpu.with_memory_space_constraint(x, pltpu.HBM)


def swap(x, count, bits):
    return lax.ppermute(x, "col", [(i, i ^ bits) for i in range(count)])


def gathered(x, count):
    found = {0: x}
    bit = count // 2
    while bit:
        for k, v in list(found.items()):
            found[k ^ bit] = swap(v, count, bit)
        bit //= 2
    return [found[k] for k in range(count)]


def spread(values, count):
    found = [values[0]]
    for k in range(1, count):
        found.append(swap(values[k], count, k))
    return found


def call(kernel, out_shape, in_specs, scratch=(), cost=10**6):
    single = not isinstance(out_shape, tuple)
    return pl.pallas_call(
        kernel,
        out_shape=out_shape,
        in_specs=in_specs,
        out_specs=VMEM if single else (VMEM,) * len(out_shape),
        scratch_shapes=scratch,
        compiler_params=pltpu.CompilerParams(vmem_limit_bytes=GRANT),
        cost_estimate=pl.CostEstimate(flops=cost, bytes_accessed=cost, transcendentals=0),
    )


def on_device(links, tiles, local_links, host_ids, dangling, teleport):
    rows, cols = lax.axis_size("row"), lax.axis_size("col")
    pages = host_ids.shape[0]
    s = Sizes(rows, cols, links.shape, tiles.shape, local_links.shape, teleport.shape, pages)
    hosts = host_ids.reshape(pages // LANES, LANES)
    ignored = dangling.reshape(pages // LANES, LANES)
    shape = jax.ShapeDtypeStruct
    sent, own, *chunks = call(
        functools.partial(first_kernel, s),
        (
            shape((rows, s.payload, LANES), bf16),
            shape((s.piece + s.packed, LANES), bf16),
            *(shape((s.piece, s.width), bf16) for _ in range(cols)),
        ),
        [HBM] * 6,
        [pltpu.SMEM(tiles.shape, tiles.dtype)]
        + [pltpu.VMEM(a.shape, a.dtype) for a in (links, hosts, ignored, local_links, teleport)]
        + [pltpu.SemaphoreType.DMA((6,))],
    )(*(in_hbm(x) for x in (tiles, links, hosts, ignored, local_links, teleport)))
    moves = [(r * cols + c, c * rows + r) for r in range(rows) for c in range(cols)]
    own = lax.ppermute(own, ("row", "col"), moves)
    chunks = spread(chunks, cols)
    group = [s.row_at(p) for p in range(rows)]
    held = lax.all_to_all(sent, "row", 0, 0, tiled=True, axis_index_groups=[group])
    local = call(functools.partial(ranks_kernel, s), shape((s.width, s.topics), bf16), [VMEM])(held)
    locals_ = gathered(local, cols)
    shared = call(
        functools.partial(graph_kernel, s),
        shape((s.column_hosts + s.extra, s.hosts), bf16),
        [VMEM] * 3,
    )(held, hosts, local)
    shared = spread([shared] * cols, cols)
    mask = call(
        functools.partial(mask_kernel, s), shape((s.piece, s.tile), f32), [VMEM] * 2
    )(hosts, ignored)
    edges = call(
        functools.partial(edges_kernel, s),
        shape((s.piece, pages), bf16),
        [VMEM] * (2 + cols),
    )(own, mask, *chunks)
    weighted, base = call(
        functools.partial(host_kernel, s),
        (shape((s.piece, pages), bf16), shape((s.piece, s.topics), f32)),
        [VMEM] * (3 + cols),
        [pltpu.VMEM((s.hosts, s.hosts), bf16), pltpu.VMEM((s.units * cols, LANES), f32)],
    )(own, hosts, edges, *shared)
    late = [k for k in range(cols) if k % 2 and k > 1]
    soon = [k for k in range(cols) if k not in late]
    flow = base
    for distances in (soon, late):
        flow = call(
            functools.partial(flow_kernel, s, distances),
            shape((s.piece, s.topics), f32),
            [VMEM] * (2 + len(distances)),
        )(weighted, flow, *(locals_[k] for k in distances))
    return flow


def solution(mesh):
    return jax.shard_map(
        on_device,
        mesh=mesh,
        in_specs=(
            P("row", "col"),
            P("row", "col"),
            P(("col", "row"), None),
            P(),
            P(),
            P(("col", "row"), None),
        ),
        out_specs=P(("row", "col"), None),
        check_vma=False,
    )
```

```python
import functools

import jax
import jax.numpy as jnp
from jax import lax
from jax.experimental import pallas as pl
from jax.experimental.pallas import tpu as pltpu
from jax.sharding import PartitionSpec as P


HOSTS_PIECE = 4
LOCAL_ITERS = 2
HOST_ITERS = 3
LANES = 128
ROW_ORDERS = {8: (4, 0, 7, 5, 3, 1, 6, 2)}
GRANT = 24 * 2**20

damping = 0.85
f32 = jnp.float32
bf16 = jnp.bfloat16

VMEM = pl.BlockSpec(memory_space=pltpu.VMEM)
SMEM = pl.BlockSpec(memory_space=pltpu.SMEM)
HBM = pl.BlockSpec(memory_space=pltpu.HBM)


def iota(shape, axis):
    return lax.broadcasted_iota(jnp.int32, shape, axis)


def mm(a, b):
    return jnp.dot(a, b, preferred_element_type=f32)


def mm_nt(a, b):
    return lax.dot_general(a, b, (((1,), (1,)), ((), ())), preferred_element_type=f32)


def mm_tn(a, b):
    return lax.dot_general(a, b, (((0,), (0,)), ((), ())), preferred_element_type=f32)


def split(x):
    high = x.astype(bf16)
    return high, (x - high.astype(f32)).astype(bf16)


def members(hosts_row, first, count):
    return hosts_row == first + iota((count, hosts_row.shape[1]), 0)


class Sizes:
    def __init__(self, rows, cols, links, tiles, local_links, teleport, pages):
        self.rows, self.cols, self.pages = rows, cols, pages
        self.height, self.width = links
        self.piece = local_links[0]
        self.topics = teleport[1]
        self.tile = self.height // tiles[0]
        self.tile_rows, self.units = tiles
        self.pair = self.tile // self.piece
        self.unit_hosts = self.pair * HOSTS_PIECE
        self.hosts = HOSTS_PIECE * rows * cols
        self.column_hosts = HOSTS_PIECE * rows
        self.row_hosts = HOSTS_PIECE * cols
        self.packed = self.piece * self.piece // LANES
        self.at_counts = self.piece
        self.at_extra = self.at_counts + self.units * self.row_hosts
        self.payload = self.at_extra + 8
        self.extra = (2 * self.units + 2 + 15) // 16 * 16

    def row_at(self, place):
        listed = ROW_ORDERS.get(self.rows)
        return listed[place] if listed else (place + self.rows // 2) % self.rows

    def place_of(self, row):
        return [self.row_at(place) for place in range(self.rows)].index(row)


def rows_of(row, half, piece):
    rolled = pltpu.roll(row, piece, 1)
    low = iota(row.shape, 1) < piece
    first = jnp.where(low, row, rolled)
    second = jnp.where(low, rolled, row)
    return jnp.where(half == 0, first, second)


def first_kernel(s, tiles_hbm, links_hbm, hosts_hbm, dangling_hbm, local_hbm, teleport_hbm, *refs):
    sent_hbm, own_ref, chunk_refs = refs[0], refs[1], refs[2 : 2 + s.cols]
    tiles_ref, links_ref, hosts_ref, dangling_ref, local_ref, teleport_ref = refs[2 + s.cols : -3]
    values_ref, sem, sent_sem = refs[-3:]
    copies = [
        pltpu.make_async_copy(source, target, sem.at[i])
        for i, (source, target) in enumerate(
            (
                (hosts_hbm, hosts_ref),
                (dangling_hbm, dangling_ref),
                (local_hbm, local_ref),
                (teleport_hbm, teleport_ref),
                (links_hbm, links_ref),
                (tiles_hbm, tiles_ref),
            )
        )
    ]
    for copy in copies:
        copy.start()
    row, column = lax.axis_index("row"), lax.axis_index("col")
    for copy in copies[:4]:
        copy.wait()
    piece = column * s.rows + row
    unit, half = piece // s.pair, piece % s.pair
    hosts = rows_of(hosts_ref[pl.ds(unit, 1), :], half, s.piece)[:, : s.piece]
    keep = rows_of(dangling_ref[pl.ds(unit, 1), :], half, s.piece)[:, : s.piece] == 0
    member = members(hosts, piece * HOSTS_PIECE, 8).astype(bf16)
    same = mm_tn(member, member)
    sameb = same.astype(bf16)
    local = local_ref[...].astype(f32)
    inside = local * same * keep.astype(f32)
    inward = jnp.sum(inside, axis=0, keepdims=True)
    size = jnp.sum(same, axis=0, keepdims=True)
    live = inward > 0
    step = inside * jnp.where(live, 1.0 / jnp.where(live, inward, 1.0), 0.0)
    step = step + same * jnp.where(live, 0.0, 1.0 / size)
    high, low = split(step)
    teleport = teleport_ref[...]
    tele_high, tele_low = split(teleport)
    sizes = jnp.sum(same, axis=1, keepdims=True)
    restart = sizes * teleport / (mm(sameb, tele_high) + mm(sameb, tele_low))
    ranks = damping * jnp.sum(step, axis=1, keepdims=True) + (1 - damping) * restart
    for _ in range(LOCAL_ITERS - 1):
        ranks_high, ranks_low = split(ranks)
        flow = mm(high, ranks_high) + mm(high, ranks_low) + mm(low, ranks_high)
        ranks = damping * flow + (1 - damping) * restart
    parts = (slice(0, s.piece), slice(s.piece, s.payload))
    sends = [
        pltpu.make_async_copy(values_ref.at[:, part], sent_hbm.at[:, part], sent_sem.at[i])
        for i, part in enumerate(parts)
    ]
    ranks = ranks.astype(bf16)
    for n in range(s.rows):
        values_ref[n, parts[0], :] = ranks
    sends[0].start()
    half_piece = s.piece // 2
    packed = jnp.concatenate([local[:half_piece], local[half_piece:]], axis=1).astype(bf16)
    own_ref[: s.piece, :] = tele_high
    own_ref[s.piece :, :] = packed
    total = jnp.sum(teleport, axis=0, keepdims=True)
    total_high = total.astype(bf16).astype(f32)
    where = iota((8, LANES), 0)
    inward = jnp.concatenate([inward, inward], axis=1)
    extra = jnp.where(where == 0, inward, jnp.where(where == 1, total_high, total - total_high))

    for copy in copies[4:]:
        copy.wait()
    counts = [[] for _ in range(s.units)]
    for a in range(s.tile_rows):
        tile_row = row * s.tile_rows + a
        first = tile_row * s.unit_hosts
        member = members(hosts_ref[pl.ds(tile_row, 1), :], first, s.unit_hosts)
        sums = mm(member.astype(bf16), links_ref[a * s.tile : (a + 1) * s.tile, :])
        for b in range(s.units):
            unit = column * s.units + b
            target = hosts_ref[pl.ds(unit, 1), :]
            valid = ~members(target, first, s.unit_hosts) & (dangling_ref[pl.ds(unit, 1), :] == 0)
            stored = (tiles_ref[a, b] > 0).astype(f32)
            part = sums[:, b * s.tile : (b + 1) * s.tile]
            counts[b].append(jnp.where(valid, part, 0.0) * stored)
    values = jnp.concatenate(
        [jnp.concatenate(c, axis=0).astype(bf16) for c in counts] + [extra.astype(bf16)], axis=0
    )
    for n in range(s.rows):
        values_ref[n, parts[1], :] = values
    sends[1].start()
    for k in range(s.cols):
        chunk = column ^ k
        at = pl.multiple_of(chunk * s.piece, s.piece)
        for b in range(s.units):
            lanes = slice(b * s.tile, (b + 1) * s.tile)
            stored = (tiles_ref[chunk // s.pair, b] > 0).astype(f32).astype(bf16)
            chunk_refs[k][:, lanes] = links_ref[pl.ds(at, s.piece), lanes] * stored
    for copy in sends:
        copy.wait()


def ranks_kernel(s, buffer_ref, local_ref):
    for n in range(s.rows):
        local_ref[n * s.piece : (n + 1) * s.piece, :] = buffer_ref[s.place_of(n), : s.piece, :]


def graph_kernel(s, buffer_ref, hosts_ref, local_ref, shared_ref):
    column = lax.axis_index("col")
    low = iota((1, LANES), 1) < s.piece
    extras = [buffer_ref[s.place_of(n), s.at_extra :, :].astype(f32) for n in range(s.rows)]
    total = functools.reduce(jnp.add, [e[1:2] + e[2:3] for e in extras])
    square = (s.tile, s.tile)
    diagonal = iota(square, 0) == iota(square, 1)
    lines = []
    for m in range(s.units):
        unit = column * s.units + m
        member = members(hosts_ref[pl.ds(unit, 1), :], unit * s.unit_hosts, s.unit_hosts)
        start = s.at_counts + m * s.row_hosts
        counts = jnp.concatenate(
            [buffer_ref[s.place_of(n), start : start + s.row_hosts, :] for n in range(s.rows)], axis=0
        )
        extra = jnp.where(low, extras[s.pair * m], extras[s.pair * m + 1])
        outward = jnp.sum(counts.astype(f32), axis=0, keepdims=True)
        degree = extra[:1] + outward
        has_out = degree > 0
        inverse = jnp.where(has_out, 1.0 / jnp.where(has_out, degree, 1.0), 0.0)
        ranks = local_ref[m * s.tile : (m + 1) * s.tile, :].astype(f32)
        sums = jnp.sum(ranks, axis=1, keepdims=True)
        sums = jnp.sum(jnp.where(diagonal, sums, 0.0), axis=0, keepdims=True)
        means = sums * (1.0 / s.topics) * inverse
        spread = (member.astype(f32) * means).astype(bf16)
        weights = mm_nt(spread, counts)
        out = jnp.sum(spread.astype(f32) * outward, axis=1, keepdims=True)
        linked = out > 0
        norm = jnp.where(linked, weights * (1.0 / jnp.where(linked, out, 1.0)), 1.0 / s.hosts)
        shared_ref[m * s.unit_hosts : (m + 1) * s.unit_hosts, :] = norm.astype(bf16)
        high = inverse.astype(bf16).astype(f32)
        lines += [high, inverse - high]
    high = total.astype(bf16).astype(f32)
    lines += [high, total - high]
    lines += [jnp.zeros((1, LANES), f32)] * (s.extra - len(lines))
    shared_ref[s.column_hosts :, :LANES] = jnp.concatenate(lines, axis=0).astype(bf16)


def mask_kernel(s, hosts_ref, dangling_ref, out_ref):
    piece = lax.axis_index("row") * s.cols + lax.axis_index("col")
    unit, half = piece // s.pair, piece % s.pair
    hosts = hosts_ref[pl.ds(unit, 1), :]
    keep = dangling_ref[pl.ds(unit, 1), :] == 0
    mine = rows_of(hosts, half, s.piece)[:, : s.piece]
    first = piece * HOSTS_PIECE
    same = mm_tn(members(mine, first, 8).astype(bf16), members(hosts, first, 8).astype(bf16))
    out_ref[...] = same * jnp.where(keep, 1.0, -1.0)


def edges_kernel(s, own_ref, mask_ref, *refs):
    chunk_refs, out_ref = refs[: s.cols], refs[s.cols]
    column = lax.axis_index("col")
    for k in range(s.cols):
        at = pl.multiple_of((column ^ k) * s.width, s.width)
        out_ref[:, pl.ds(at, s.width)] = chunk_refs[k][...]
    unit = (lax.axis_index("row") * s.cols + column) // s.pair
    mask = mask_ref[...]
    packed = own_ref[s.piece :, :].astype(f32)
    rolled = pltpu.roll(packed, s.piece, 1)
    low = iota((s.packed, LANES), 1) < s.piece
    local = jnp.concatenate([jnp.where(low, packed, rolled), jnp.where(low, rolled, packed)], axis=0)
    at = pl.multiple_of(unit * s.tile, s.tile)
    across = out_ref[:, pl.ds(at, s.tile)].astype(f32)
    fixed = jnp.where(mask == 0, across, jnp.where(mask > 0, local, 0.0))
    out_ref[:, pl.ds(at, s.tile)] = fixed.astype(bf16)


def three(x):
    high = x.astype(bf16).astype(f32)
    rest = x - high
    middle = rest.astype(bf16).astype(f32)
    where = iota((8, x.shape[1]), 0)
    parts = jnp.where(where == 0, high, jnp.where(where == 1, middle, rest - middle))
    return jnp.where(where < 3, parts, 0.0).astype(bf16)


def host_kernel(s, own_ref, hosts_ref, edges_ref, *refs):
    shared, (weighted_ref, base_ref, full_ref, inverse_ref) = refs[: s.cols], refs[s.cols :]
    column = lax.axis_index("col")
    total = jnp.zeros((1, s.topics), f32)
    for k in range(s.cols):
        at = pl.multiple_of((column ^ k) * s.column_hosts, s.column_hosts)
        full_ref[pl.ds(at, s.column_hosts), :] = shared[k][: s.column_hosts, :]
        lines = shared[k][s.column_hosts :, :LANES].astype(f32)
        for m in range(s.units):
            line = lines[2 * m : 2 * m + 1] + lines[2 * m + 1 : 2 * m + 2]
            inverse_ref[pl.ds((column ^ k) * s.units + m, 1), :] = line
        total = total + lines[2 * s.units : 2 * s.units + 1] + lines[2 * s.units + 1 : 2 * s.units + 2]
    base_ref[...] = (1 - damping) * s.pages * own_ref[: s.piece, :].astype(f32) / total
    norm = full_ref[...]
    parts = jnp.where(iota((8, s.hosts), 0) == 0, 1.0, 0.0).astype(bf16)
    for step in range(HOST_ITERS):
        if step:
            parts = three(rank)
        rank = damping * jnp.sum(mm(parts, norm), axis=0, keepdims=True) + (1 - damping)
    block = LANES // s.unit_hosts
    all_units = s.units * s.cols
    for g in range(s.hosts // LANES):
        count = min(block, all_units - g * block)
        hosts = hosts_ref[g * block : g * block + count, :] - g * LANES
        ranks = jnp.broadcast_to(rank[:, g * LANES : (g + 1) * LANES], (count, LANES))
        page = damping * jnp.take_along_axis(ranks, hosts, axis=1)
        inverse = inverse_ref[g * block : g * block + count, :]
        scale = page * inverse
        dead = jnp.where(inverse > 0, 0.0, page * (1.0 / s.pages))
        for u in range(count):
            at = (g * block + u) * s.tile
            lanes = slice(at, at + s.tile)
            links = edges_ref[:, lanes].astype(f32)
            weighted_ref[:, lanes] = (links * scale[u : u + 1] + dead[u : u + 1]).astype(bf16)


def flow_kernel(s, distances, weighted_ref, base_ref, *refs):
    locals_, out_ref = refs[:-1], refs[-1]
    column = lax.axis_index("col")
    flow = base_ref[...]
    for k, local_ref in zip(distances, locals_, strict=True):
        at = pl.multiple_of((column ^ k) * s.width, s.width)
        flow = flow + mm(weighted_ref[:, pl.ds(at, s.width)], local_ref[...])
    out_ref[...] = flow


def in_hbm(x):
    return pltpu.with_memory_space_constraint(x, pltpu.HBM)


def swap(x, count, bits):
    return lax.ppermute(x, "col", [(i, i ^ bits) for i in range(count)])


def gathered(x, count):
    found = {0: x}
    bit = count // 2
    while bit:
        for k, v in list(found.items()):
            found[k ^ bit] = swap(v, count, bit)
        bit //= 2
    return [found[k] for k in range(count)]


def spread(values, count):
    found = [values[0]]
    for k in range(1, count):
        found.append(swap(values[k], count, k))
    return found


def call(kernel, out_shape, in_specs, scratch=(), cost=10**6, out_specs=None):
    if out_specs is None:
        out_specs = (VMEM,) * len(out_shape) if isinstance(out_shape, tuple) else VMEM
    return pl.pallas_call(
        kernel,
        out_shape=out_shape,
        in_specs=in_specs,
        out_specs=out_specs,
        scratch_shapes=scratch,
        compiler_params=pltpu.CompilerParams(vmem_limit_bytes=GRANT),
        cost_estimate=pl.CostEstimate(flops=cost, bytes_accessed=cost, transcendentals=0),
    )


def on_device(links, tiles, local_links, host_ids, dangling, teleport):
    rows, cols = lax.axis_size("row"), lax.axis_size("col")
    pages = host_ids.shape[0]
    s = Sizes(rows, cols, links.shape, tiles.shape, local_links.shape, teleport.shape, pages)
    hosts = host_ids.reshape(pages // LANES, LANES)
    ignored = dangling.reshape(pages // LANES, LANES)
    shape = jax.ShapeDtypeStruct
    sent, own, *chunks = call(
        functools.partial(first_kernel, s),
        (
            pltpu.HBM((rows, s.payload, LANES), bf16),
            shape((s.piece + s.packed, LANES), bf16),
            *(shape((s.piece, s.width), bf16) for _ in range(cols)),
        ),
        [HBM] * 6,
        [pltpu.SMEM(tiles.shape, tiles.dtype)]
        + [pltpu.VMEM(a.shape, a.dtype) for a in (links, hosts, ignored, local_links, teleport)]
        + [pltpu.VMEM((rows, s.payload, LANES), bf16)]
        + [pltpu.SemaphoreType.DMA((6,)), pltpu.SemaphoreType.DMA((2,))],
        out_specs=(HBM,) + (VMEM,) * (1 + cols),
    )(*(in_hbm(x) for x in (tiles, links, hosts, ignored, local_links, teleport)))
    moves = [(r * cols + c, c * rows + r) for r in range(rows) for c in range(cols)]
    own = lax.ppermute(own, ("row", "col"), moves)
    chunks = spread(chunks, cols)
    group = [s.row_at(p) for p in range(rows)]
    held = lax.all_to_all(sent, "row", 0, 0, tiled=True, axis_index_groups=[group])
    local = call(functools.partial(ranks_kernel, s), shape((s.width, s.topics), bf16), [VMEM])(held)
    locals_ = gathered(local, cols)
    shared = call(
        functools.partial(graph_kernel, s),
        shape((s.column_hosts + s.extra, s.hosts), bf16),
        [VMEM] * 3,
    )(held, hosts, local)
    shared = spread([shared] * cols, cols)
    mask = call(
        functools.partial(mask_kernel, s), shape((s.piece, s.tile), f32), [VMEM] * 2
    )(hosts, ignored)
    edges = call(
        functools.partial(edges_kernel, s),
        shape((s.piece, pages), bf16),
        [VMEM] * (2 + cols),
    )(own, mask, *chunks)
    weighted, base = call(
        functools.partial(host_kernel, s),
        (shape((s.piece, pages), bf16), shape((s.piece, s.topics), f32)),
        [VMEM] * (3 + cols),
        [pltpu.VMEM((s.hosts, s.hosts), bf16), pltpu.VMEM((s.units * cols, LANES), f32)],
    )(own, hosts, edges, *shared)
    late = [k for k in range(cols) if k % 2 and k > 1]
    soon = [k for k in range(cols) if k not in late]
    flow = base
    for distances in (soon, late):
        flow = call(
            functools.partial(flow_kernel, s, distances),
            shape((s.piece, s.topics), f32),
            [VMEM] * (2 + len(distances)),
        )(weighted, flow, *(locals_[k] for k in distances))
    return flow


def solution(mesh):
    return jax.shard_map(
        on_device,
        mesh=mesh,
        in_specs=(
            P("row", "col"),
            P("row", "col"),
            P(("col", "row"), None),
            P(),
            P(),
            P(("col", "row"), None),
        ),
        out_specs=P(("row", "col"), None),
        check_vma=False,
    )
```
